256 devices in a mesh: kv: 8 (over z_lo, x), bead: 32 (over y, z_hi, core).
Axes of the slice: x: 4, y: 4, z: 8 (z_hi: 4, z_lo: 2; z = z_hi * 2 + z_lo), core: 2. Of those that a mesh axis runs over, the one named last changes fastest.
Arguments:
- miller: int32 [3, 8192], P(None, 'kv'), may hold values from -40 to 40
- lattice_pos: int32 [3, 32768], P(None, ('kv', 'bead')), may hold values from 0 to 4095
- weights: float32 [32, 32768], P(None, ('kv', 'bead')), may hold values from -6 to 6
- observed: float32 [32, 8192], P(None, 'kv'), may hold values from 0.3 to 2
Outputs:
- grad_weights: float32 [32, 32768], P(None, ('kv', 'bead'))
- grad_positions: float32 [3, 32768], P(None, ('kv', 'bead'))
The draws below stay inside these ranges and needn't reach their ends.
All inputs are finite; a program needn't handle non-finite values.
Results may differ from the reference program's by a relative error of at most 0.0003.
Values sent between devices are 32-bit elements; how exact they have to be, the bound alone decides.
A program may use at most 64 MiB of HBM per device.

```python
import math
import jax
import jax.numpy as jnp
from jax import lax

CHANNELS = 32
LATTICE = 4096
MILLER_MAX = 40
BOX_LEN = 64
BEADS = 32768
WAVES = 8192


def with_ends(result, key, low, high):
    extent = result.shape
    spot = [jax.random.randint(jax.random.fold_in(key, axis), (), 0, extent[axis]) for axis in range(len(extent))]
    result = result.at[tuple(spot)].set(low)
    longest = extent.index(max(extent))
    spot[longest] = (spot[longest] + 1) % extent[longest]
    return result.at[tuple(spot)].set(high)


def level_of(own_key, dims, split, low, high):
    level, own = 1.0, jax.random.fold_in(own_key, 6)
    for position, blocks in split:
        heights = jnp.exp(jax.random.uniform(jax.random.fold_in(own, position), (blocks,), jnp.float32, low / len(split), high / len(split)))
        level = level * jnp.repeat(heights, dims[position] // blocks).reshape([-1 if axis == position else 1 for axis in range(len(dims))])
    return level


def centred(rng, extent, spread, limit, cuts=(), dtype=jnp.bfloat16):
    array = jax.random.normal(rng, extent, jnp.float32) * spread
    if len(cuts) > 0:
        array = level_of(rng, extent, cuts, -0.22, 0.18) * array
    return jnp.clip(array, min=-limit, max=limit).astype(dtype)


def setup_inputs(seed: int = 0) -> dict:
    keys = jax.random.split(jax.random.key(seed), 5)
    miller = with_ends(jax.random.randint(keys[0], (3, WAVES), 0 - MILLER_MAX, MILLER_MAX + 1), jax.random.fold_in(keys[0], 1), 0 - MILLER_MAX, MILLER_MAX).astype(jnp.int32)
    lattice_pos = with_ends(jax.random.randint(keys[1], (3, BEADS), 0, LATTICE), jax.random.fold_in(keys[1], 1), 0, LATTICE - 1).astype(jnp.int32)
    weights = centred(keys[2], (CHANNELS, BEADS), 1.0, 6.0, ((1, 256),), jnp.float32)
    observed = jnp.clip(0.3 + 1.7 * jax.random.uniform(keys[3], (CHANNELS, WAVES), jnp.float32) ** level_of(keys[3], (CHANNELS, WAVES), ((1, 8),), -0.2, 0.2), 0.3, 2.0)
    return {"miller": miller, "lattice_pos": lattice_pos, "weights": weights, "observed": observed}


HIGH = lax.Precision.HIGHEST
TWO_PI = 2.0 * math.pi


def phases(mil_block, positions):
    integer = mil_block[0][:, None] * positions[0][None, :]
    integer = integer + mil_block[1][:, None] * positions[1][None, :]
    integer = integer + mil_block[2][:, None] * positions[2][None, :]
    return jnp.mod(integer, LATTICE).astype(jnp.float32) * (TWO_PI / LATTICE)


def reference(miller, lattice_pos, weights, observed):
    wave_count = miller.shape[1]
    block_size = math.gcd(wave_count, 512)
    count_blocks = wave_count // block_size
    mil_blocks = miller.reshape(3, count_blocks, block_size).transpose(1, 0, 2)

    def forward(mil_block):
        angles = phases(mil_block, lattice_pos)
        first = jnp.dot(weights, jnp.cos(angles).T, precision=HIGH, preferred_element_type=jnp.float32)
        second = jnp.dot(weights, jnp.sin(angles).T, precision=HIGH, preferred_element_type=jnp.float32)
        return first, second

    cos_blocks, sin_blocks = lax.map(forward, mil_blocks)
    amp_cos = cos_blocks.transpose(1, 0, 2).reshape(CHANNELS, wave_count)
    amp_sin = sin_blocks.transpose(1, 0, 2).reshape(CHANNELS, wave_count)
    bead_total = lattice_pos.shape[1]
    residual = (amp_cos * amp_cos + amp_sin * amp_sin) / bead_total - observed
    coef_cos = 2.0 * residual * amp_cos / bead_total
    coef_sin = 2.0 * residual * amp_sin / bead_total
    wave_vec = miller.astype(jnp.float32) * (TWO_PI / BOX_LEN)
    left_cos = jnp.concatenate([coef_cos] + [wave_vec[comp][None, :] * coef_sin for comp in range(3)], 0)
    left_sin = jnp.concatenate([coef_sin] + [-wave_vec[comp][None, :] * coef_cos for comp in range(3)], 0)
    left_cos = left_cos.reshape(4 * CHANNELS, count_blocks, block_size).transpose(1, 0, 2)
    left_sin = left_sin.reshape(4 * CHANNELS, count_blocks, block_size).transpose(1, 0, 2)

    def advance(running, pieces):
        mil_block, cos_left, sin_left = pieces
        angles = phases(mil_block, lattice_pos)
        running = running + jnp.dot(cos_left, jnp.cos(angles), precision=HIGH, preferred_element_type=jnp.float32)
        running = running + jnp.dot(sin_left, jnp.sin(angles), precision=HIGH, preferred_element_type=jnp.float32)
        return running, None

    start_total = jnp.zeros((4 * CHANNELS, bead_total), jnp.float32)
    summed, unused = lax.scan(advance, start_total, (mil_blocks, left_cos, left_sin))
    grad_weights = summed[:CHANNELS]
    grad_positions = jnp.stack([jnp.sum(weights * summed[CHANNELS * (comp + 1):CHANNELS * (comp + 2)], 0) for comp in range(3)])
    return grad_weights, grad_positions
```

```python
import functools
import math

import jax
import jax.numpy as jnp
from jax import lax
from jax.experimental import pallas as pl
from jax.experimental.pallas import tpu as pltpu
from jax.sharding import PartitionSpec as P

CHANNELS = 32
LATTICE = 4096
BOX_LEN = 64
TWO_PI = 2.0 * math.pi
MESH = pl.DeviceIdType.MESH
BF16 = jnp.bfloat16
F32 = jnp.float32

SIN_POLY = (4.442883014678955, -7.308241367340088, 3.6062889099121094, -0.8457635641098022, 0.10920574516057968)
COS_POLY = (1.4142135381698608, -6.978850841522217, 5.7394609451293945, -1.8835629224777222, 0.31069815158843994)

GROUP = 16
CHUNK = 128
NT = (((1,), (1,)), ((), ()))
NN = (((1,), (0,)), ((), ()))


def poly(u, coefs):
    total = u * coefs[-1] + coefs[-2]
    for c in coefs[-3::-1]:
        total = total * u + c
    return total


def cos_sin(turns):
    f = turns - jnp.round(turns)
    u = f * f
    s = poly(u, SIN_POLY) * f
    c = poly(u, COS_POLY)
    return 1.0 - s * s, s * c


def split(x):
    high = x.astype(BF16)
    return high, (x - high.astype(F32)).astype(BF16)


def dot(a, b, dims):
    return lax.dot_general(a, b, dims, preferred_element_type=F32)


def kernel(
    mil, pos, wts, obs, gw_out, gp_out,
    posbuf, wbuf, mil_t, wsplit, phase, cos_hi, cos_lo, sin_hi, sin_lo,
    amps, shares, coefs, left_cos, left_sin, gw_send, gp_send, gw_recv, gp_recv,
    a_send, a_recv, r_send, r_recv, c_send, c_recv, d_send, d_recv,
):
    kv, bead = lax.axis_index("kv"), lax.axis_index("bead")
    core, yz = lax.rem(bead, 2), bead // 2
    own = kv * 2 + core
    waves = mil.shape[1] // 2
    beads = pos.shape[1]
    half = pl.ds(pl.multiple_of(core * waves, waves), waves)

    def bead_peer(g):
        return (g // 2, yz * 2 + lax.rem(g, 2))

    def wave_peer(j):
        return (kv, j * 2 + core)

    def turned(index, shift):
        return lax.rem(index + shift, GROUP)

    def lanes(g):
        return pl.ds(pl.multiple_of(g * beads, beads), beads)

    def remote(src, dst, send, recv, device):
        return pltpu.make_async_remote_copy(
            src_ref=src, dst_ref=dst, send_sem=send, recv_sem=recv, device_id=device, device_id_type=MESH
        )

    barrier = pltpu.get_barrier_semaphore()
    for s in range(1, GROUP):
        pl.semaphore_signal(barrier, inc=1, device_id=bead_peer(turned(own, s)), device_id_type=MESH)
    for s in range(1, GROUP):
        pl.semaphore_signal(barrier, inc=1, device_id=wave_peer(turned(yz, s)), device_id_type=MESH)

    where = pos[...].astype(F32)
    upper = jnp.floor(where * (1.0 / 64.0))
    lower = where - 64.0 * upper
    posbuf[:, lanes(own)] = jnp.concatenate(
        [upper * (1.0 / 64.0), lower * (1.0 / LATTICE), jnp.zeros((2, beads), F32)], 0
    )
    wbuf[:, lanes(own)] = wts[...]

    pl.semaphore_wait(barrier, 2 * (GROUP - 1))

    pos_copies, wts_copies = [], []
    for s in range(1, GROUP):
        copy = remote(
            posbuf.at[:, lanes(own)], posbuf.at[:, lanes(own)],
            a_send.at[0, s], a_recv.at[0, s], bead_peer(turned(own, s)),
        )
        copy.start()
        pos_copies.append(copy)
    for s in range(1, GROUP):
        copy = remote(
            wbuf.at[:, lanes(own)], wbuf.at[:, lanes(own)],
            a_send.at[1, s], a_recv.at[1, s], bead_peer(turned(own, s)),
        )
        copy.start()
        wts_copies.append(copy)

    index = mil[:, half].astype(F32)
    mil_t[...] = jnp.concatenate([index, index, jnp.zeros((2, waves), F32)], 0).T.astype(BF16)

    for copy in pos_copies:
        copy.wait_recv()
    for copy in wts_copies:
        copy.wait_recv()
    high, low = split(wbuf[...])
    wsplit[...] = jnp.concatenate([high, low], 0)

    rows, columns = 32, 256

    def forward(q, carry):
        first = pl.multiple_of(q * CHUNK, CHUNK)
        phase[...] = dot(mil_t[pl.ds(first, CHUNK), :], posbuf[...].astype(BF16), NN)

        def block(i, inner):
            r = pl.multiple_of(i * rows, rows)
            to = pl.ds(pl.multiple_of(first + r, rows), rows)
            for j in range(phase.shape[1] // columns):
                c = slice(j * columns, (j + 1) * columns)
                co, si = cos_sin(phase[pl.ds(r, rows), c])
                cos_hi[to, c], cos_lo[to, c] = split(co)
                sin_hi[to, c], sin_lo[to, c] = split(si)
            return inner

        lax.fori_loop(0, CHUNK // rows, block, 0)
        here = pl.ds(first, CHUNK)
        for part, (e_hi, e_lo) in enumerate(((cos_hi, cos_lo), (sin_hi, sin_lo))):
            both = dot(wsplit[...], e_hi[here, :], NT)
            amp = both[:CHANNELS] + both[CHANNELS:] + dot(wsplit[:CHANNELS, :], e_lo[here, :], NT)
            for j in range(GROUP):
                amps[j, 2 * part : 2 * part + 1, here] = amp[j : j + 1]
                amps[j, 2 * part + 1 : 2 * part + 2, here] = amp[GROUP + j : GROUP + j + 1]
        for s in range(1, GROUP):
            to = turned(yz, s)
            remote(
                amps.at[to, :, here], shares.at[yz, :, here], r_send.at[q, s], r_recv.at[q, s], wave_peer(to)
            ).start()
        return carry

    lax.fori_loop(0, waves // CHUNK, forward, 0)
    shares[yz] = amps[yz]

    def share_copy(q, s):
        to, here = turned(yz, s), pl.ds(q * CHUNK, CHUNK)
        return remote(
            amps.at[to, :, here], shares.at[yz, :, here], r_send.at[q, s], r_recv.at[q, s], wave_peer(to)
        )

    for q in range(waves // CHUNK):
        for s in range(1, GROUP):
            share_copy(q, s).wait_recv()
    total = shares[0]
    for j in range(1, GROUP):
        total = total + shares[j]
    bead_total = float(CHANNELS * 1024)
    amp_cos, amp_sin = total[0:2], total[2:4]
    measured = jnp.concatenate([obs[pl.ds(yz, 1), half], obs[pl.ds(yz + GROUP, 1), half]], 0)
    residual = (amp_cos * amp_cos + amp_sin * amp_sin) * (1.0 / bead_total) - measured
    scale = residual * (2.0 / bead_total)
    coefs[yz] = jnp.concatenate([scale * amp_cos, scale * amp_sin], 0)

    coef_copies = []
    for s in range(1, GROUP):
        copy = remote(coefs.at[yz], coefs.at[yz], c_send.at[s], c_recv.at[s], wave_peer(turned(yz, s)))
        copy.start()
        coef_copies.append(copy)
    for copy in coef_copies:
        copy.wait_recv()

    every = coefs[...]
    coef_cos = jnp.concatenate([every[:, 0, :], every[:, 1, :]], 0)
    coef_sin = jnp.concatenate([every[:, 2, :], every[:, 3, :]], 0)
    wave_vec = mil[:, half].astype(F32) * (TWO_PI / BOX_LEN)
    for d in range(4):
        if d == 0:
            lc, ls = coef_cos, coef_sin
        else:
            lc, ls = wave_vec[d - 1 : d] * coef_sin, -wave_vec[d - 1 : d] * coef_cos
        for left, value in ((left_cos, lc), (left_sin, ls)):
            hi, lo = split(value)
            left[d * CHANNELS : (d + 1) * CHANNELS, :] = hi
            left[(4 + d) * CHANNELS : (5 + d) * CHANNELS, :] = lo

    wide = 4 * CHANNELS

    def sum_copies(s):
        to = turned(own, s)
        return (
            remote(gw_send.at[to], gw_recv.at[own], d_send.at[0, s], d_recv.at[0, s], bead_peer(to)),
            remote(gp_send.at[to], gp_recv.at[own], d_send.at[1, s], d_recv.at[1, s], bead_peer(to)),
        )

    def backward(i, carry):
        chip = lax.rem(kv + 1 + i, 8)
        at = pl.ds(pl.multiple_of(chip * 2 * beads, 2 * beads), 2 * beads)
        total = None
        for left, e_hi, e_lo in ((left_cos, cos_hi, cos_lo), (left_sin, sin_hi, sin_lo)):
            both = dot(left[...], e_hi[:, at], NN)
            part = both[:wide] + both[wide:] + dot(left[:wide, :], e_lo[:, at], NN)
            total = part if total is None else total + part
        weight = wbuf[:, at]
        comps = [
            jnp.sum(weight * total[CHANNELS * (d + 1) : CHANNELS * (d + 2)], 0, keepdims=True) for d in range(3)
        ]
        comps = jnp.concatenate(comps + [jnp.zeros((1, 2 * beads), F32)], 0)
        for c in range(2):
            g = chip * 2 + c
            gw_send[g] = total[:CHANNELS, c * beads : (c + 1) * beads]
            gp_send[g] = comps[:, c * beads : (c + 1) * beads]

            @pl.when(g != own)
            def _():
                s = lax.rem(g - own + GROUP, GROUP)
                for copy in (
                    remote(gw_send.at[g], gw_recv.at[own], d_send.at[0, s], d_recv.at[0, s], bead_peer(g)),
                    remote(gp_send.at[g], gp_recv.at[own], d_send.at[1, s], d_recv.at[1, s], bead_peer(g)),
                ):
                    copy.start()

        return carry

    lax.fori_loop(0, 8, backward, 0)
    gw_recv[own] = gw_send[own]
    gp_recv[own] = gp_send[own]
    for s in range(1, GROUP):
        for copy in sum_copies(s):
            copy.wait_recv()
    gw, gp = gw_recv[0], gp_recv[0]
    for g in range(1, GROUP):
        gw, gp = gw + gw_recv[g], gp + gp_recv[g]
    gw_out[...] = gw
    gp_out[...] = gp[:3]

    for copy in pos_copies + wts_copies + coef_copies:
        copy.wait_send()
    for s in range(1, GROUP):
        for q in range(waves // CHUNK):
            share_copy(q, s).wait_send()
        for copy in sum_copies(s):
            copy.wait_send()


def per_device(miller, lattice_pos, weights, observed):
    waves, beads = miller.shape[1] // 2, lattice_pos.shape[1]
    many = GROUP * beads
    chunks = waves // CHUNK
    vmem = pl.BlockSpec(memory_space=pltpu.VMEM)
    dma = pltpu.SemaphoreType.DMA
    return pl.pallas_call(
        kernel,
        out_shape=(
            jax.ShapeDtypeStruct((CHANNELS, beads), F32),
            jax.ShapeDtypeStruct((3, beads), F32),
        ),
        in_specs=[vmem] * 4,
        out_specs=[vmem] * 2,
        scratch_shapes=[
            pltpu.VMEM((8, many), F32),
            pltpu.VMEM((CHANNELS, many), F32),
            pltpu.VMEM((waves, 8), BF16),
            pltpu.VMEM((2 * CHANNELS, many), BF16),
            pltpu.VMEM((CHUNK, many), F32),
            pltpu.VMEM((waves, many), BF16),
            pltpu.VMEM((waves, many), BF16),
            pltpu.VMEM((waves, many), BF16),
            pltpu.VMEM((waves, many), BF16),
            pltpu.VMEM((GROUP, 4, waves), F32),
            pltpu.VMEM((GROUP, 4, waves), F32),
            pltpu.VMEM((GROUP, 4, waves), F32),
            pltpu.VMEM((8 * CHANNELS, waves), BF16),
            pltpu.VMEM((8 * CHANNELS, waves), BF16),
            pltpu.VMEM((GROUP, CHANNELS, beads), F32),
            pltpu.VMEM((GROUP, 4, beads), F32),
            pltpu.VMEM((GROUP, CHANNELS, beads), F32),
            pltpu.VMEM((GROUP, 4, beads), F32),
            dma((2, GROUP)),
            dma((2, GROUP)),
            dma((chunks, GROUP)),
            dma((chunks, GROUP)),
            dma((GROUP,)),
            dma((GROUP,)),
            dma((2, GROUP)),
            dma((2, GROUP)),
        ],
        compiler_params=pltpu.CompilerParams(
            collective_id=0, has_side_effects=True, vmem_limit_bytes=48 * 1024 * 1024
        ),
    )(miller, lattice_pos, weights, observed)


def solution(mesh):
    in_specs = (P(None, "kv"), P(None, ("kv", "bead")), P(None, ("kv", "bead")), P(None, "kv"))
    out_specs = (P(None, ("kv", "bead")), P(None, ("kv", "bead")))
    return jax.shard_map(
        per_device, mesh=mesh, in_specs=in_specs, out_specs=out_specs, check_vma=False
    )
```

```python
import functools
import math

import jax
import jax.numpy as jnp
from jax import lax
from jax.experimental import pallas as pl
from jax.experimental.pallas import tpu as pltpu
from jax.sharding import PartitionSpec as P

CHANNELS = 32
LATTICE = 4096
BOX_LEN = 64
TWO_PI = 2.0 * math.pi
MESH = pl.DeviceIdType.MESH
BF16 = jnp.bfloat16
F32 = jnp.float32

SIN_POLY = (4.442883014678955, -7.308241367340088, 3.6062889099121094, -0.8457635641098022, 0.10920574516057968)
COS_POLY = (1.4142135381698608, -6.978850841522217, 5.7394609451293945, -1.8835629224777222, 0.31069815158843994)

SHARERS = 8
REDUCERS = 32
CHUNK = 256
SLICE = 256
TILES = CHUNK // 128
PIECE = 2 * TILES
FIRST_GROUP = 2
NT = (((1,), (1,)), ((), ()))
NN = (((1,), (0,)), ((), ()))


def poly(u, coefs):
    total = u * coefs[-1] + coefs[-2]
    for c in coefs[-3::-1]:
        total = total * u + c
    return total


def cos_sin(turns):
    f = turns - jnp.round(turns)
    u = f * f
    s = poly(u, SIN_POLY) * f
    c = poly(u, COS_POLY)
    return 1.0 - s * s, s * c


def split(x):
    high = x.astype(BF16)
    return high, (x - high.astype(F32)).astype(BF16)


def dot(a, b, dims):
    return lax.dot_general(a, b, dims, preferred_element_type=F32)


def kernel(
    mil, pos, wts, obs, gw_out, gp_out,
    mil_own, mil_use, pos_own, obs_own, obs_row, obs_send, posbuf, wbuf, mil_t, wsplit,
    even_ch, even_cl, even_sh, even_sl, odd_ch, odd_cl, odd_sh, odd_sl,
    amps, shares, coefs, left_cos, left_sin, grads, gw_send, gp_send, gw_recv, gp_recv,
    in_sem, a_send, a_recv, m_send, m_recv, r_send, r_recv, c_send, c_recv, d_send, d_recv,
    ready, met,
):
    kv, bead = lax.axis_index("kv"), lax.axis_index("bead")
    z_low, x = kv // 4, lax.rem(kv, 4)
    core = lax.rem(bead, 2)
    own = x * 2 + core
    channel = (bead // 8) * 8 + lax.rem(bead // 2, 4) * 2 + z_low
    waves, beads = mil_use.shape[1], pos.shape[1]
    chunks = waves // CHUNK
    chips = SHARERS // 2
    pairs = chips // 2

    def sharer(g):
        return (z_low * 4 + g // 2, (bead // 2) * 2 + lax.rem(g, 2))

    def reducer(r, to_core):
        y, z = r // 8, lax.rem(r, 8)
        return (lax.rem(z, 2) * 4 + x, (y * 4 + z // 2) * 2 + to_core)

    def remote(src, dst, send, recv, device):
        return pltpu.make_async_remote_copy(
            src_ref=src, dst_ref=dst, send_sem=send, recv_sem=recv, device_id=device, device_id_type=MESH
        )

    def greet(device):
        pl.semaphore_signal(barrier, inc=1, device_id=device, device_id_type=MESH)

    def lanes(g):
        return pl.ds(pl.multiple_of(g * beads, beads), beads)

    barrier = pltpu.get_barrier_semaphore()
    for s in range(1, chips):
        greet(sharer(2 * lax.rem(x + s, chips)))

    @pl.when(core == 1)
    def _():
        greet((kv, bead - 1))

    greet(((1 - z_low) * 4 + x, bead - core))
    inputs = [
        pltpu.make_async_copy(src, dst, in_sem.at[i])
        for i, (src, dst) in enumerate(
            ((pos, pos_own), (wts, wbuf.at[:, lanes(own)]), (mil, mil_own), (obs, obs_own))
        )
    ]
    for copy in inputs:
        copy.start()
    for s in range(1, REDUCERS):
        greet(reducer(lax.rem(channel + s, REDUCERS), 1))
    for copy in inputs:
        copy.wait()

    where = pos_own[...].astype(F32)
    upper = jnp.floor(where * (1.0 / 64.0))
    lower = where - 64.0 * upper
    posbuf[:, lanes(own)] = jnp.concatenate(
        [upper * (1.0 / 64.0), lower * (1.0 / LATTICE), jnp.zeros((2, beads), F32)], 0
    )

    def put_row(ref, row):
        for t in range(waves // 128):
            ref[t : t + 1, :] = row[:, t * 128 : (t + 1) * 128]

    @pl.when(core == 0)
    def _():
        put_row(obs_send, obs_own[pl.ds(channel + 1 - 2 * z_low, 1), :])

    @pl.when(core == z_low)
    def _():
        mil_use[...] = mil_own[...]
        put_row(obs_row, obs_own[pl.ds(channel, 1), :])

    @pl.when(core == 0)
    def _():
        pl.semaphore_wait(barrier, SHARERS - 1 + 2)
        pl.semaphore_signal(ready, inc=1, device_id=(kv, bead + 1), device_id_type=MESH)

    @pl.when(core == 1)
    def _():
        pl.semaphore_wait(ready, 1)

    def pos_copy(s):
        g = lax.rem(own + s, SHARERS)
        at = posbuf.at[:, lanes(own)]
        return remote(at, at, a_send.at[0, s], a_recv.at[0, s], sharer(g))

    def wts_copy(s):
        g = lax.rem(own + s, SHARERS)
        at = wbuf.at[:, lanes(own)]
        return remote(at, at, a_send.at[1, s], a_recv.at[1, s], sharer(g))

    beyond = ((1 - z_low) * 4 + x, bead - core + z_low)
    mil_copy = remote(mil_own, mil_use, m_send.at[0], m_recv.at[0], beyond)
    obs_copy = remote(obs_send, obs_row, m_send.at[1], m_recv.at[1], beyond)

    for s in range(1, SHARERS):
        pos_copy(s).start()

    @pl.when(core == 0)
    def _():
        mil_copy.start()
        obs_copy.start()

    for s in range(1, SHARERS):
        wts_copy(s).start()

    @pl.when(core != z_low)
    def _():
        mil_copy.wait_recv()

    index = mil_use[...].astype(F32)
    mil_t[...] = jnp.concatenate([index, index, jnp.zeros((2, waves), F32)], 0).T.astype(BF16)

    for s in range(1, SHARERS):
        pos_copy(s).wait_recv()
    for s in range(1, SHARERS):
        wts_copy(s).wait_recv()
    high, low = split(wbuf[...])
    wsplit[...] = jnp.concatenate([high, low], 0)

    even = ((even_ch, even_cl), (even_sh, even_sl))
    odd = ((odd_ch, odd_cl), (odd_sh, odd_sl))
    rows = 32

    def share_copy(q, r, to):
        src = amps.at[q, pl.ds(pl.multiple_of(to * PIECE, PIECE), PIECE), :]
        dst = shares.at[q, pl.ds(pl.multiple_of(r * PIECE, PIECE), PIECE), :]
        return remote(src, dst, r_send.at[q], r_recv.at[q], reducer(to, core))

    def coef_copy(q, to):
        at = coefs.at[q, pl.ds(pl.multiple_of(channel * PIECE, PIECE), PIECE), :]
        return remote(at, at, c_send.at[q], c_recv.at[q], reducer(to, core))

    def all_pieces(buf, q, send, recv):
        at = buf.at[q, pl.ds(0, (REDUCERS - 1) * PIECE), :]
        return remote(at, at, send.at[q], recv.at[q], reducer(lax.rem(channel + 1, REDUCERS), core))

    def forward(q, carry):
        first = pl.multiple_of(q * CHUNK, CHUNK)
        mine = mil_t[pl.ds(first, CHUNK), :]

        def make(i):
            refs = (even, odd)[i % 2]
            at = slice((i // 2) * SLICE, (i // 2 + 1) * SLICE)
            where = posbuf[:, i * SLICE : (i + 1) * SLICE].astype(BF16)
            turns = dot(mine, where, NN)
            for b in range(CHUNK // rows):
                to = pl.ds(pl.multiple_of(first + b * rows, rows), rows)
                for (hi, lo), value in zip(refs, cos_sin(turns[b * rows : (b + 1) * rows])):
                    hi[to, at], lo[to, at] = split(value)

        def add(i, sums):
            refs = (even, odd)[i % 2]
            at = slice((i // 2) * SLICE, (i // 2 + 1) * SLICE)
            w = wsplit[:, i * SLICE : (i + 1) * SLICE]
            here = pl.ds(first, CHUNK)
            out = []
            for (hi, lo), (both, rest) in zip(refs, sums):
                both = both + dot(w, hi[here, at], NT)
                rest = rest + dot(w[:CHANNELS], lo[here, at], NT)
                out.append((both, rest))
            return out

        slices = SHARERS * beads // SLICE
        sums = [(jnp.zeros((2 * CHANNELS, CHUNK), F32), jnp.zeros((CHANNELS, CHUNK), F32))] * 2
        make(0)
        for i in range(1, slices):
            make(i)
            sums = add(i - 1, sums)
        sums = add(slices - 1, sums)
        for part, (both, rest) in enumerate(sums):
            amp = both[:CHANNELS] + both[CHANNELS:] + rest
            for t in range(TILES):
                amps[q, pl.ds(part * TILES + t, REDUCERS, stride=PIECE), :] = amp[:, t * 128 : (t + 1) * 128]

        @pl.when(jnp.logical_and(q == 0, core == 1))
        def _():
            pl.semaphore_wait(barrier, 2 * (REDUCERS - 1))
            pl.semaphore_signal(met, inc=1, device_id=(kv, bead - 1), device_id_type=MESH)

        @pl.when(jnp.logical_and(q == 0, core == 0))
        def _():
            pl.semaphore_wait(met, 1)

        for s in range(1, REDUCERS):
            share_copy(q, channel, lax.rem(channel + s, REDUCERS)).start()
        own_rows = pl.ds(pl.multiple_of(channel * PIECE, PIECE), PIECE)
        shares[q, own_rows, :] = amps[q, own_rows, :]
        return carry

    lax.fori_loop(0, chunks, forward, 0)

    @pl.when(core != z_low)
    def _():
        obs_copy.wait_recv()

    bead_total = float(CHANNELS * 1024)

    def coefficients(q, carry):
        all_pieces(shares, q, r_send, r_recv).wait_recv()
        total = shares[q, 0:8, :]
        for r in range(8, REDUCERS * PIECE, 8):
            total = total + shares[q, r : r + 8, :]
        total = total[:PIECE] + total[PIECE:]
        amp_cos, amp_sin = total[:TILES], total[TILES:]
        measured = obs_row[pl.ds(q * TILES, TILES), :]
        residual = (amp_cos * amp_cos + amp_sin * amp_sin) * (1.0 / bead_total) - measured
        scale = residual * (2.0 / bead_total)
        own_rows = pl.ds(pl.multiple_of(channel * PIECE, PIECE), PIECE)
        coefs[q, own_rows, :] = jnp.concatenate([scale * amp_cos, scale * amp_sin], 0)
        for s in range(1, REDUCERS):
            coef_copy(q, lax.rem(channel + s, REDUCERS)).start()
        return carry

    lax.fori_loop(0, chunks, coefficients, 0)

    wide = 4 * CHANNELS

    def sum_copies(g, s):
        device = sharer(g)
        return (
            remote(gw_send.at[g], gw_recv.at[own], d_send.at[0, s], d_recv.at[0, s], device),
            remote(gp_send.at[g], gp_recv.at[own], d_send.at[1, s], d_recv.at[1, s], device),
        )

    def backward(begin, end):
        span = slice(begin * CHUNK, end * CHUNK)
        for q in range(begin, end):
            all_pieces(coefs, q, c_send, c_recv).wait_recv()
            for t in range(TILES):
                at = slice(q * CHUNK + t * 128, q * CHUNK + (t + 1) * 128)
                co = coefs[q, pl.ds(t, CHANNELS, stride=PIECE), :]
                si = coefs[q, pl.ds(TILES + t, CHANNELS, stride=PIECE), :]
                vec = mil_use[:, at].astype(F32) * (TWO_PI / BOX_LEN)
                for d in range(4):
                    lc, ls = (co, si) if d == 0 else (vec[d - 1 : d] * si, -vec[d - 1 : d] * co)
                    for left, value in ((left_cos, lc), (left_sin, ls)):
                        hi, lo = split(value)
                        left[d * CHANNELS : (d + 1) * CHANNELS, at] = hi
                        left[(4 + d) * CHANNELS : (5 + d) * CHANNELS, at] = lo

        def pair(i, carry):
            m = lax.rem(x // 2 + 1 + i, pairs)
            at = pl.ds(pl.multiple_of(m * SLICE, SLICE), SLICE)
            for parity, refs in enumerate((even, odd)):
                chip = m * 2 + parity
                to = pl.ds(pl.multiple_of(chip * SLICE, SLICE), SLICE)
                total = None if begin == 0 else grads[:, to]
                for left, (hi, lo) in zip((left_cos, left_sin), refs):
                    both = dot(left[:, span], hi[span, at], NN)
                    part = both[:wide] + both[wide:] + dot(left[:wide, span], lo[span, at], NN)
                    total = part if total is None else total + part
                if end < chunks:
                    grads[:, to] = total
                    continue
                weight = wbuf[:, to]
                comps = [
                    jnp.sum(weight * total[CHANNELS * (d + 1) : CHANNELS * (d + 2)], 0, keepdims=True)
                    for d in range(3)
                ]
                comps = jnp.concatenate(comps + [jnp.zeros((1, SLICE), F32)], 0)
                for c in range(2):
                    g = chip * 2 + c
                    gw_send[g] = total[:CHANNELS, c * beads : (c + 1) * beads]
                    gp_send[g] = comps[:, c * beads : (c + 1) * beads]

                    @pl.when(g != own)
                    def _():
                        for copy in sum_copies(g, lax.rem(g - own + SHARERS, SHARERS)):
                            copy.start()

            return carry

        lax.fori_loop(0, pairs, pair, 0)

    backward(0, FIRST_GROUP)
    backward(FIRST_GROUP, chunks)

    gw_recv[own] = gw_send[own]
    gp_recv[own] = gp_send[own]
    for s in range(1, SHARERS):
        for copy in sum_copies(lax.rem(own + s, SHARERS), s):
            copy.wait_recv()
    gw, gp = gw_recv[0], gp_recv[0]
    for g in range(1, SHARERS):
        gw, gp = gw + gw_recv[g], gp + gp_recv[g]
    gw_out[...] = gw
    gp_out[...] = gp[:3]

    for s in range(1, SHARERS):
        pos_copy(s).wait_send()
        wts_copy(s).wait_send()
        for copy in sum_copies(lax.rem(own + s, SHARERS), s):
            copy.wait_send()
    for q in range(chunks):
        all_pieces(amps, q, r_send, r_recv).wait_send()
        all_pieces(coefs, q, c_send, c_recv).wait_send()

    @pl.when(core == 0)
    def _():
        mil_copy.wait_send()
        obs_copy.wait_send()


def per_device(miller, lattice_pos, weights, observed):
    waves, beads = miller.shape[1], lattice_pos.shape[1]
    many = SHARERS * beads
    chunks = waves // CHUNK
    hbm = pl.BlockSpec(memory_space=pltpu.HBM)
    vmem = pl.BlockSpec(memory_space=pltpu.VMEM)
    dma = pltpu.SemaphoreType.DMA
    pieces = pltpu.VMEM((chunks, REDUCERS * PIECE, 128), F32)
    left = pltpu.VMEM((8 * CHANNELS, waves), BF16)
    sent = [pltpu.VMEM((SHARERS, CHANNELS, beads), F32), pltpu.VMEM((SHARERS, 4, beads), F32)]
    return pl.pallas_call(
        kernel,
        out_shape=(
            jax.ShapeDtypeStruct((CHANNELS, beads), F32),
            jax.ShapeDtypeStruct((3, beads), F32),
        ),
        in_specs=[hbm] * 4,
        out_specs=[vmem] * 2,
        scratch_shapes=[
            pltpu.VMEM(miller.shape, jnp.int32),
            pltpu.VMEM(miller.shape, jnp.int32),
            pltpu.VMEM(lattice_pos.shape, jnp.int32),
            pltpu.VMEM(observed.shape, F32),
            pltpu.VMEM((waves // 128, 128), F32),
            pltpu.VMEM((waves // 128, 128), F32),
            pltpu.VMEM((8, many), F32),
            pltpu.VMEM((CHANNELS, many), F32),
            pltpu.VMEM((waves, 8), BF16),
            pltpu.VMEM((2 * CHANNELS, many), BF16),
        ]
        + [pltpu.VMEM((waves, many // 2), BF16)] * 8
        + [pieces] * 3
        + [left] * 2
        + [pltpu.VMEM((4 * CHANNELS, many), F32)]
        + sent * 2
        + [
            dma((4,)),
            dma((2, SHARERS)),
            dma((2, SHARERS)),
            dma((2,)),
            dma((2,)),
            dma((chunks,)),
            dma((chunks,)),
            dma((chunks,)),
            dma((chunks,)),
            dma((2, SHARERS)),
            dma((2, SHARERS)),
            pltpu.SemaphoreType.REGULAR,
            pltpu.SemaphoreType.REGULAR,
        ],
        compiler_params=pltpu.CompilerParams(
            collective_id=0, has_side_effects=True, vmem_limit_bytes=56 * 1024 * 1024
        ),
    )(miller, lattice_pos, weights, observed)


def solution(mesh):
    in_specs = (P(None, "kv"), P(None, ("kv", "bead")), P(None, ("kv", "bead")), P(None, "kv"))
    out_specs = (P(None, ("kv", "bead")), P(None, ("kv", "bead")))
    return jax.shard_map(
        per_device, mesh=mesh, in_specs=in_specs, out_specs=out_specs, check_vma=False
    )
```

```python
import functools
import math

import jax
import jax.numpy as jnp
from jax import lax
from jax.experimental import pallas as pl
from jax.experimental.pallas import tpu as pltpu
from jax.sharding import PartitionSpec as P

CHANNELS = 32
LATTICE = 4096
BOX_LEN = 64
BEADS = 32768
TWO_PI = 2.0 * math.pi
MESH = pl.DeviceIdType.MESH
BF16 = jnp.bfloat16
F32 = jnp.float32

SIN_POLY = (4.442883014678955, -7.308241367340088, 3.6062889099121094, -0.8457635641098022, 0.10920574516057968)
COS_POLY = (1.4142135381698608, -6.978850841522217, 5.7394609451293945, -1.8835629224777222, 0.31069815158843994)

SHARERS = 8
REDUCERS = 32
CHUNK = 256
SLICE = 256
TILES = CHUNK // 128
PIECE = 2 * TILES
NT = (((1,), (1,)), ((), ()))
NN = (((1,), (0,)), ((), ()))


def poly(u, coefs):
    total = u * coefs[-1] + coefs[-2]
    for c in coefs[-3::-1]:
        total = total * u + c
    return total


def cos_sin(turns):
    f = turns - jnp.round(turns)
    u = f * f
    s = poly(u, SIN_POLY) * f
    c = poly(u, COS_POLY)
    return 1.0 - s * s, s * c


def split(x):
    high = x.astype(BF16)
    return high, (x - high.astype(F32)).astype(BF16)


def dot(a, b, dims):
    return lax.dot_general(a, b, dims, preferred_element_type=F32)


def kernel(
    mil, pos, wts, obs, gw_out, gp_out,
    mil_own, mil_use, pos_own, obs_own, obs_row, obs_send, posbuf, wbuf, mil_rows, pos_t, wsplit,
    hi_a, lo_a, hi_b, lo_b, phase,
    amps, shares, coefs, left, grads, gw_send, gp_send, gw_recv, gp_recv,
    in_sem, a_send, a_recv, m_send, m_recv, r_send, r_recv, c_send, c_recv, d_send, d_recv,
    ready, met,
):
    kv, bead = lax.axis_index("kv"), lax.axis_index("bead")
    z_low, x = kv // 4, lax.rem(kv, 4)
    core = lax.rem(bead, 2)
    own = x * 2 + core
    channel = (bead // 8) * 8 + lax.rem(bead // 2, 4) * 2 + z_low
    waves, beads = mil_use.shape[1], pos.shape[1]
    chunks = waves // CHUNK
    chips = SHARERS // 2

    def sharer(g):
        return (z_low * 4 + g // 2, (bead // 2) * 2 + lax.rem(g, 2))

    def reducer(r, to_core):
        y, z = r // 8, lax.rem(r, 8)
        return (lax.rem(z, 2) * 4 + x, (y * 4 + z // 2) * 2 + to_core)

    def remote(src, dst, send, recv, device):
        return pltpu.make_async_remote_copy(
            src_ref=src, dst_ref=dst, send_sem=send, recv_sem=recv, device_id=device, device_id_type=MESH
        )

    def greet(device):
        pl.semaphore_signal(barrier, inc=1, device_id=device, device_id_type=MESH)

    def lanes(g):
        return pl.ds(pl.multiple_of(g * beads, beads), beads)

    barrier = pltpu.get_barrier_semaphore()
    for s in range(1, chips):
        greet(sharer(2 * lax.rem(x + s, chips)))

    @pl.when(core == 1)
    def _():
        greet((kv, bead - 1))

    greet(((1 - z_low) * 4 + x, bead - core))
    inputs = [
        pltpu.make_async_copy(src, dst, in_sem.at[i])
        for i, (src, dst) in enumerate(
            ((pos, pos_own), (wts, wbuf.at[:, lanes(own)]), (mil, mil_own), (obs, obs_own))
        )
    ]
    for copy in inputs:
        copy.start()
    for copy in inputs:
        copy.wait()

    where = pos_own[...].astype(F32)
    upper = jnp.floor(where * (1.0 / 64.0))
    lower = where - 64.0 * upper
    posbuf[:, lanes(own)] = jnp.concatenate(
        [upper * (1.0 / 64.0), lower * (1.0 / LATTICE), jnp.zeros((2, beads), F32)], 0
    )

    def put_row(ref, row):
        for t in range(waves // 128):
            ref[t : t + 1, :] = row[:, t * 128 : (t + 1) * 128]

    @pl.when(core == 0)
    def _():
        put_row(obs_send, obs_own[pl.ds(channel + 1 - 2 * z_low, 1), :])

    @pl.when(core == z_low)
    def _():
        mil_use[...] = mil_own[...]
        put_row(obs_row, obs_own[pl.ds(channel, 1), :])

    @pl.when(core == 0)
    def _():
        pl.semaphore_wait(barrier, SHARERS - 1 + 2)
        pl.semaphore_signal(ready, inc=1, device_id=(kv, bead + 1), device_id_type=MESH)

    @pl.when(core == 1)
    def _():
        pl.semaphore_wait(ready, 1)

    def pos_copy(s):
        g = lax.rem(own + s, SHARERS)
        at = posbuf.at[:, lanes(own)]
        return remote(at, at, a_send.at[0, s], a_recv.at[0, s], sharer(g))

    def wts_copy(s):
        g = lax.rem(own + s, SHARERS)
        at = wbuf.at[:, lanes(own)]
        return remote(at, at, a_send.at[1, s], a_recv.at[1, s], sharer(g))

    beyond = ((1 - z_low) * 4 + x, bead - core + z_low)
    mil_copy = remote(mil_own, mil_use, m_send.at[0], m_recv.at[0], beyond)
    obs_copy = remote(obs_send, obs_row, m_send.at[1], m_recv.at[1], beyond)

    for s in range(1, SHARERS):
        pos_copy(s).start()

    @pl.when(core == 0)
    def _():
        mil_copy.start()
        obs_copy.start()

    for s in range(1, SHARERS):
        wts_copy(s).start()
    for s in range(1, REDUCERS):
        greet(reducer(lax.rem(channel + s, REDUCERS), 1))

    @pl.when(core != z_low)
    def _():
        mil_copy.wait_recv()

    index = mil_use[...].astype(F32)
    mil_rows[...] = jnp.concatenate([index, index, jnp.zeros((2, waves), F32)], 0).astype(BF16)

    for s in range(1, SHARERS):
        pos_copy(s).wait_recv()
    pos_t[...] = posbuf[...].T.astype(BF16)

    sets = ((hi_a, lo_a), (hi_b, lo_b))
    rows = 32

    def share_copy(q, r, to):
        src = amps.at[q, pl.ds(pl.multiple_of(to * PIECE, PIECE), PIECE), :]
        dst = shares.at[q, pl.ds(pl.multiple_of(r * PIECE, PIECE), PIECE), :]
        return remote(src, dst, r_send.at[q], r_recv.at[q], reducer(to, core))

    def coef_copy(q, to):
        at = coefs.at[q, pl.ds(pl.multiple_of(channel * PIECE, PIECE), PIECE), :]
        return remote(at, at, c_send.at[q], c_recv.at[q], reducer(to, core))

    def all_pieces(buf, q, send, recv):
        at = buf.at[q, pl.ds(0, (REDUCERS - 1) * PIECE), :]
        return remote(at, at, send.at[q], recv.at[q], reducer(lax.rem(channel + 1, REDUCERS), core))

    def add(q, turn, base):
        hi, lo = sets[turn]
        at = pl.ds(base, 2 * CHUNK)
        both = dot(wsplit[...], hi[:, at], NN)
        amp = both[:CHANNELS] + both[CHANNELS:] + dot(wsplit[:CHANNELS, :], lo[:, at], NN)
        for t in range(PIECE):
            amps[q, pl.ds(t, REDUCERS, stride=PIECE), :] = amp[:, t * 128 : (t + 1) * 128]

    def make(q, turn, base):
        hi, lo = sets[turn]
        phase[...] = dot(pos_t[...], mil_rows[:, pl.ds(pl.multiple_of(q * CHUNK, CHUNK), CHUNK)], NN)
        for r in range(0, phase.shape[0], rows):
            for part, value in enumerate(cos_sin(phase[r : r + rows, :])):
                at = pl.ds(pl.multiple_of(base + part * CHUNK, CHUNK), CHUNK)
                hi[r : r + rows, at], lo[r : r + rows, at] = split(value)

    def send_shares(q):
        for s in range(1, REDUCERS):
            share_copy(q, channel, lax.rem(channel + s, REDUCERS)).start()
        own_rows = pl.ds(pl.multiple_of(channel * PIECE, PIECE), PIECE)
        shares[q, own_rows, :] = amps[q, own_rows, :]

    def forward(h, carry):
        base = pl.multiple_of(h * 2 * CHUNK, 2 * CHUNK)
        before = pl.multiple_of(jnp.maximum(h - 1, 0) * 2 * CHUNK, 2 * CHUNK)
        add(lax.rem(2 * h + chunks - 1, chunks), 1, before)
        make(2 * h, 0, base)

        @pl.when(h > 0)
        def _():
            send_shares(2 * h - 1)

        @pl.when(h == 0)
        def _():
            for s in range(1, SHARERS):
                wts_copy(s).wait_recv()
            high, low = split(wbuf[...])
            wsplit[...] = jnp.concatenate([high, low], 0)

        add(2 * h, 0, base)
        make(2 * h + 1, 1, base)

        @pl.when(jnp.logical_and(h == 0, core == 1))
        def _():
            pl.semaphore_wait(barrier, 2 * (REDUCERS - 1))
            pl.semaphore_signal(met, inc=1, device_id=(kv, bead - 1), device_id_type=MESH)

        @pl.when(jnp.logical_and(h == 0, core == 0))
        def _():
            pl.semaphore_wait(met, 1)

        send_shares(2 * h)
        return carry

    lax.fori_loop(0, chunks // 2, forward, 0)
    add(chunks - 1, 1, (chunks // 2 - 1) * 2 * CHUNK)
    send_shares(chunks - 1)

    @pl.when(core != z_low)
    def _():
        obs_copy.wait_recv()

    bead_total = float(BEADS)

    def coefficients(q, carry):
        all_pieces(shares, q, r_send, r_recv).wait_recv()
        total = shares[q, 0:8, :]
        for r in range(8, REDUCERS * PIECE, 8):
            total = total + shares[q, r : r + 8, :]
        total = total[:PIECE] + total[PIECE:]
        amp_cos, amp_sin = total[:TILES], total[TILES:]
        measured = obs_row[pl.ds(q * TILES, TILES), :]
        residual = (amp_cos * amp_cos + amp_sin * amp_sin) * (1.0 / bead_total) - measured
        scale = residual * (2.0 / bead_total)
        own_rows = pl.ds(pl.multiple_of(channel * PIECE, PIECE), PIECE)
        coefs[q, own_rows, :] = jnp.concatenate([scale * amp_cos, scale * amp_sin], 0)
        for s in range(1, REDUCERS):
            coef_copy(q, lax.rem(channel + s, REDUCERS)).start()
        return carry

    lax.fori_loop(0, chunks, coefficients, 0)

    wide = 4 * CHANNELS

    def sum_copies(g, s):
        device = sharer(g)
        return (
            remote(gw_send.at[g], gw_recv.at[own], d_send.at[0, s], d_recv.at[0, s], device),
            remote(gp_send.at[g], gp_recv.at[own], d_send.at[1, s], d_recv.at[1, s], device),
        )

    def backward(h):
        for q in (2 * h, 2 * h + 1):
            all_pieces(coefs, q, c_send, c_recv).wait_recv()
            for t in range(TILES):
                at = slice(q * CHUNK + t * 128, q * CHUNK + (t + 1) * 128)
                co = coefs[q, pl.ds(t, CHANNELS, stride=PIECE), :]
                si = coefs[q, pl.ds(TILES + t, CHANNELS, stride=PIECE), :]
                vec = mil_use[:, at].astype(F32) * (TWO_PI / BOX_LEN)
                for d in range(4):
                    lc, ls = (co, si) if d == 0 else (vec[d - 1 : d] * si, -vec[d - 1 : d] * co)
                    for part, value in ((0, lc), (1, ls)):
                        hi, lo = split(value)
                        first = (2 * (q - 2 * h) + part) * CHUNK + t * 128
                        to = slice(first, first + 128)
                        left[d * CHANNELS : (d + 1) * CHANNELS, to] = hi
                        left[(4 + d) * CHANNELS : (5 + d) * CHANNELS, to] = lo

        span = slice(h * 2 * CHUNK, (h + 1) * 2 * CHUNK)

        def one_chip(i, carry):
            chip = lax.rem(x + 1 + i, chips)
            at = pl.ds(pl.multiple_of(chip * SLICE, SLICE), SLICE)
            both = dot(left[...], jnp.concatenate([hi_a[at, span], hi_b[at, span]], 1), NT)
            rest = dot(left[:wide, :], jnp.concatenate([lo_a[at, span], lo_b[at, span]], 1), NT)
            total = both[:wide] + both[wide:] + rest
            if h > 0:
                total = total + grads[:, at]
            if h < chunks // 2 - 1:
                grads[:, at] = total
                return carry
            weight = wbuf[:, at]
            comps = [
                jnp.sum(weight * total[CHANNELS * (d + 1) : CHANNELS * (d + 2)], 0, keepdims=True) for d in range(3)
            ]
            comps = jnp.concatenate(comps + [jnp.zeros((1, SLICE), F32)], 0)
            for c in range(2):
                g = chip * 2 + c
                gw_send[g] = total[:CHANNELS, c * beads : (c + 1) * beads]
                gp_send[g] = comps[:, c * beads : (c + 1) * beads]

                @pl.when(g != own)
                def _():
                    for copy in sum_copies(g, lax.rem(g - own + SHARERS, SHARERS)):
                        copy.start()

            return carry

        lax.fori_loop(0, chips, one_chip, 0)

    for h in range(chunks // 2):
        backward(h)

    gw_recv[own] = gw_send[own]
    gp_recv[own] = gp_send[own]
    for s in range(1, SHARERS):
        for copy in sum_copies(lax.rem(own + s, SHARERS), s):
            copy.wait_recv()
    gw, gp = gw_recv[0], gp_recv[0]
    for g in range(1, SHARERS):
        gw, gp = gw + gw_recv[g], gp + gp_recv[g]
    gw_out[...] = gw
    gp_out[...] = gp[:3]

    for s in range(1, SHARERS):
        pos_copy(s).wait_send()
        wts_copy(s).wait_send()
        for copy in sum_copies(lax.rem(own + s, SHARERS), s):
            copy.wait_send()
    for q in range(chunks):
        all_pieces(amps, q, r_send, r_recv).wait_send()
        all_pieces(coefs, q, c_send, c_recv).wait_send()

    @pl.when(core == 0)
    def _():
        mil_copy.wait_send()
        obs_copy.wait_send()


def per_device(miller, lattice_pos, weights, observed):
    waves, beads = miller.shape[1], lattice_pos.shape[1]
    many = SHARERS * beads
    chunks = waves // CHUNK
    hbm = pl.BlockSpec(memory_space=pltpu.HBM)
    vmem = pl.BlockSpec(memory_space=pltpu.VMEM)
    dma = pltpu.SemaphoreType.DMA
    pieces = pltpu.VMEM((chunks, REDUCERS * PIECE, 128), F32)
    sent = [pltpu.VMEM((SHARERS, CHANNELS, beads), F32), pltpu.VMEM((SHARERS, 4, beads), F32)]
    return pl.pallas_call(
        kernel,
        out_shape=(
            jax.ShapeDtypeStruct((CHANNELS, beads), F32),
            jax.ShapeDtypeStruct((3, beads), F32),
        ),
        in_specs=[hbm] * 4,
        out_specs=[vmem] * 2,
        scratch_shapes=[
            pltpu.VMEM(miller.shape, jnp.int32),
            pltpu.VMEM(miller.shape, jnp.int32),
            pltpu.VMEM(lattice_pos.shape, jnp.int32),
            pltpu.VMEM(observed.shape, F32),
            pltpu.VMEM((waves // 128, 128), F32),
            pltpu.VMEM((waves // 128, 128), F32),
            pltpu.VMEM((8, many), F32),
            pltpu.VMEM((CHANNELS, many), F32),
            pltpu.VMEM((8, waves), BF16),
            pltpu.VMEM((many, 8), BF16),
            pltpu.VMEM((2 * CHANNELS, many), BF16),
        ]
        + [pltpu.VMEM((many, waves), BF16)] * 4
        + [pltpu.VMEM((many, CHUNK), F32)]
        + [pieces] * 3
        + [pltpu.VMEM((8 * CHANNELS, 4 * CHUNK), BF16), pltpu.VMEM((4 * CHANNELS, many), F32)]
        + sent * 2
        + [
            dma((4,)),
            dma((2, SHARERS)),
            dma((2, SHARERS)),
            dma((2,)),
            dma((2,)),
            dma((chunks,)),
            dma((chunks,)),
            dma((chunks,)),
            dma((chunks,)),
            dma((2, SHARERS)),
            dma((2, SHARERS)),
            pltpu.SemaphoreType.REGULAR,
            pltpu.SemaphoreType.REGULAR,
        ],
        compiler_params=pltpu.CompilerParams(
            collective_id=0, has_side_effects=True, vmem_limit_bytes=56 * 1024 * 1024
        ),
    )(miller, lattice_pos, weights, observed)


def solution(mesh):
    in_specs = (P(None, "kv"), P(None, ("kv", "bead")), P(None, ("kv", "bead")), P(None, "kv"))
    out_specs = (P(None, ("kv", "bead")), P(None, ("kv", "bead")))
    return jax.shard_map(
        per_device, mesh=mesh, in_specs=in_specs, out_specs=out_specs, check_vma=False
    )
```

```python
import functools
import math

import jax
import jax.numpy as jnp
from jax import lax
from jax.experimental import pallas as pl
from jax.experimental.pallas import tpu as pltpu
from jax.sharding import PartitionSpec as P

CHANNELS = 32
LATTICE = 4096
BOX_LEN = 64
BEADS = 32768
TWO_PI = 2.0 * math.pi
MESH = pl.DeviceIdType.MESH
BF16 = jnp.bfloat16
F32 = jnp.float32

SIN_POLY = (4.442883014678955, -7.308241367340088, 3.6062889099121094, -0.8457635641098022, 0.10920574516057968)

SHARERS = 8
REDUCERS = 32
CHUNK = 256
SLICE = 256
TILES = CHUNK // 128
PIECE = 2 * TILES
NT = (((1,), (1,)), ((), ()))
NN = (((1,), (0,)), ((), ()))


FAR_FIRST = sorted(
    ((dy, dz) for dy in range(4) for dz in range(8) if dy or dz),
    key=lambda step: -min(step[0], 4 - step[0]) - min(step[1], 8 - step[1]),
)


def poly(u, coefs):
    total = u * coefs[-1] + coefs[-2]
    for c in coefs[-3::-1]:
        total = total * u + c
    return total


def cos_sin(turns):
    f = turns - jnp.round(turns)
    u = f * f
    s = poly(u, SIN_POLY) * f
    square = s * s
    rest = jnp.maximum(2.0 - square, 1e-30)
    return 1.0 - square, s * (rest * lax.rsqrt(rest))


def split(x):
    high = x.astype(BF16)
    return high, (x - high.astype(F32)).astype(BF16)


def dot(a, b, dims):
    return lax.dot_general(a, b, dims, preferred_element_type=F32)


def kernel(
    mil, pos, wts, obs, gw_recv, gp_recv,
    mil_own, mil_use, pos_own, obs_own, obs_row, obs_send, posbuf, wbuf, mil_rows, pos_t, wsplit,
    hi_a, lo_a, hi_b, lo_b, phase,
    amps, shares, coefs, left, grads, gw_send, gp_send,
    in_sem, a_send, a_recv, m_send, m_recv, r_send, r_recv, c_send, c_recv, d_send, d_recv,
    ready, met,
):
    kv, bead = lax.axis_index("kv"), lax.axis_index("bead")
    z_low, x = kv // 4, lax.rem(kv, 4)
    core = lax.rem(bead, 2)
    own = x * 2 + core
    channel = (bead // 8) * 8 + lax.rem(bead // 2, 4) * 2 + z_low
    waves, beads = mil_use.shape[1], pos.shape[1]
    chunks = waves // CHUNK
    chips = SHARERS // 2

    def sharer(g):
        return (z_low * 4 + g // 2, (bead // 2) * 2 + lax.rem(g, 2))

    def reducer(r, to_core):
        y, z = r // 8, lax.rem(r, 8)
        return (lax.rem(z, 2) * 4 + x, (y * 4 + z // 2) * 2 + to_core)

    def others():
        for dy, dz in FAR_FIRST:
            yield lax.rem(channel // 8 + dy, 4) * 8 + lax.rem(channel + dz, 8)

    def remote(src, dst, send, recv, device):
        return pltpu.make_async_remote_copy(
            src_ref=src, dst_ref=dst, send_sem=send, recv_sem=recv, device_id=device, device_id_type=MESH
        )

    def greet(device):
        pl.semaphore_signal(barrier, inc=1, device_id=device, device_id_type=MESH)

    def lanes(g):
        return pl.ds(pl.multiple_of(g * beads, beads), beads)

    barrier = pltpu.get_barrier_semaphore()
    for s in range(1, chips):
        greet(sharer(2 * lax.rem(x + s, chips)))

    @pl.when(core == 1)
    def _():
        greet((kv, bead - 1))

    greet(((1 - z_low) * 4 + x, bead - core))
    inputs = [
        pltpu.make_async_copy(src, dst, in_sem.at[i])
        for i, (src, dst) in enumerate(
            ((pos, pos_own), (wts, wbuf.at[:, lanes(own)]), (mil, mil_own), (obs, obs_own))
        )
    ]
    for copy in inputs:
        copy.start()
    for s in range(1, REDUCERS):
        greet(reducer(lax.rem(channel + s, REDUCERS), 1))
    for copy in inputs:
        copy.wait()

    where = pos_own[...].astype(F32)
    upper = jnp.floor(where * (1.0 / 64.0))
    lower = where - 64.0 * upper
    posbuf[:, lanes(own)] = jnp.concatenate(
        [upper * (1.0 / 64.0), lower * (1.0 / LATTICE), jnp.zeros((2, beads), F32)], 0
    )

    def put_row(ref, row):
        for t in range(waves // 128):
            ref[t : t + 1, :] = row[:, t * 128 : (t + 1) * 128]

    @pl.when(core == 0)
    def _():
        put_row(obs_send, obs_own[pl.ds(channel + 1 - 2 * z_low, 1), :])

    @pl.when(core == z_low)
    def _():
        mil_use[...] = mil_own[...]
        put_row(obs_row, obs_own[pl.ds(channel, 1), :])

    @pl.when(core == 0)
    def _():
        pl.semaphore_wait(barrier, SHARERS - 1 + 2)
        pl.semaphore_signal(ready, inc=1, device_id=(kv, bead + 1), device_id_type=MESH)

    @pl.when(core == 1)
    def _():
        pl.semaphore_wait(ready, 1)

    def pos_copy(s):
        g = lax.rem(own + s, SHARERS)
        at = posbuf.at[:, lanes(own)]
        return remote(at, at, a_send.at[0, s], a_recv.at[0, s], sharer(g))

    def wts_copy(s):
        g = lax.rem(own + s, SHARERS)
        at = wbuf.at[:, lanes(own)]
        return remote(at, at, a_send.at[1, s], a_recv.at[1, s], sharer(g))

    beyond = ((1 - z_low) * 4 + x, bead - core + z_low)
    mil_copy = remote(mil_own, mil_use, m_send.at[0], m_recv.at[0], beyond)
    obs_copy = remote(obs_send, obs_row, m_send.at[1], m_recv.at[1], beyond)

    for s in range(1, SHARERS):
        pos_copy(s).start()

    @pl.when(core == 0)
    def _():
        mil_copy.start()
        obs_copy.start()

    for s in range(1, SHARERS):
        wts_copy(s).start()

    @pl.when(core != z_low)
    def _():
        mil_copy.wait_recv()

    index = mil_use[...].astype(F32)
    mil_rows[...] = jnp.concatenate([index, index, jnp.zeros((2, waves), F32)], 0).astype(BF16)

    sets = ((hi_a, lo_a), (hi_b, lo_b))
    rows = 32

    def share_copy(q, r, to):
        src = amps.at[q, pl.ds(pl.multiple_of(to * PIECE, PIECE), PIECE), :]
        dst = shares.at[q, pl.ds(pl.multiple_of(r * PIECE, PIECE), PIECE), :]
        return remote(src, dst, r_send.at[q], r_recv.at[q], reducer(to, core))

    def coef_copy(q, to):
        at = coefs.at[q, pl.ds(pl.multiple_of(channel * PIECE, PIECE), PIECE), :]
        return remote(at, at, c_send.at[q], c_recv.at[q], reducer(to, core))

    def all_pieces(buf, q, send, recv):
        at = buf.at[q, pl.ds(0, (REDUCERS - 1) * PIECE), :]
        return remote(at, at, send.at[q], recv.at[q], reducer(lax.rem(channel + 1, REDUCERS), core))

    def add(q, turn, base):
        hi, lo = sets[turn]
        at = slice(base, base + 2 * CHUNK)
        both = dot(wsplit[...], hi[:, at], NN)
        amp = both[:CHANNELS] + both[CHANNELS:] + dot(wsplit[:CHANNELS, :], lo[:, at], NN)
        for t in range(PIECE):
            amps[q, pl.ds(t, REDUCERS, stride=PIECE), :] = amp[:, t * 128 : (t + 1) * 128]

    def make(q, turn, base, first=0, count=SHARERS * beads):
        hi, lo = sets[turn]
        phase[0:count, :] = dot(pos_t[pl.ds(first, count), :], mil_rows[:, q * CHUNK : (q + 1) * CHUNK], NN)
        for r in range(0, count, rows):
            to = pl.ds(first + r, rows) if isinstance(first, int) else pl.ds(pl.multiple_of(first + r, rows), rows)
            for part, value in enumerate(cos_sin(phase[r : r + rows, :])):
                at = slice(base + part * CHUNK, base + (part + 1) * CHUNK)
                hi[to, at], lo[to, at] = split(value)

    def send_shares(q):
        for r in others():
            share_copy(q, channel, r).start()
        own_rows = pl.ds(pl.multiple_of(channel * PIECE, PIECE), PIECE)
        shares[q, own_rows, :] = amps[q, own_rows, :]

    for step in (0, 1, 3, 2):
        chip = lax.rem(x + step, chips)
        for c in range(2):
            g = chip * 2 + c
            shift = lax.rem(own - g + SHARERS, SHARERS)
            if step:
                pos_copy(shift).wait_recv()
            else:

                @pl.when(g != own)
                def _():
                    pos_copy(shift).wait_recv()

        here = pl.multiple_of(chip * SLICE, SLICE)
        pos_t[pl.ds(here, SLICE), :] = posbuf[:, pl.ds(here, SLICE)].T.astype(BF16)
        make(0, 0, 0, here, SLICE)

    for s in range(1, SHARERS):
        wts_copy(s).wait_recv()
    high, low = split(wbuf[...])
    wsplit[...] = jnp.concatenate([high, low], 0)

    for q in range(chunks):
        base = (q // 2) * 2 * CHUNK
        add(q, q % 2, base)
        if q + 1 < chunks:
            make(q + 1, (q + 1) % 2, ((q + 1) // 2) * 2 * CHUNK)
        if q == 0:

            @pl.when(core == 1)
            def _():
                pl.semaphore_wait(barrier, 2 * (REDUCERS - 1))
                pl.semaphore_signal(met, inc=1, device_id=(kv, bead - 1), device_id_type=MESH)

            @pl.when(core == 0)
            def _():
                pl.semaphore_wait(met, 1)

        send_shares(q)

    @pl.when(core != z_low)
    def _():
        obs_copy.wait_recv()

    bead_total = float(BEADS)

    def coefficients(q, carry):
        all_pieces(shares, q, r_send, r_recv).wait_recv()
        total = shares[q, 0:8, :]
        for r in range(8, REDUCERS * PIECE, 8):
            total = total + shares[q, r : r + 8, :]
        total = total[:PIECE] + total[PIECE:]
        amp_cos, amp_sin = total[:TILES], total[TILES:]
        measured = obs_row[pl.ds(q * TILES, TILES), :]
        residual = (amp_cos * amp_cos + amp_sin * amp_sin) * (1.0 / bead_total) - measured
        scale = residual * (2.0 / bead_total)
        own_rows = pl.ds(pl.multiple_of(channel * PIECE, PIECE), PIECE)
        coefs[q, own_rows, :] = jnp.concatenate([scale * amp_cos, scale * amp_sin], 0)
        for r in others():
            coef_copy(q, r).start()
        return carry

    lax.fori_loop(0, chunks, coefficients, 0)

    wide = 4 * CHANNELS

    def sum_copies(g, s):
        device = sharer(g)
        return (
            remote(gw_send.at[g], gw_recv.at[own], d_send.at[0, s], d_recv.at[0, s], device),
            remote(gp_send.at[g], gp_recv.at[own], d_send.at[1, s], d_recv.at[1, s], device),
        )

    def backward(h):
        for q in (2 * h, 2 * h + 1):
            all_pieces(coefs, q, c_send, c_recv).wait_recv()
            for t in range(TILES):
                at = slice(q * CHUNK + t * 128, q * CHUNK + (t + 1) * 128)
                co = coefs[q, pl.ds(t, CHANNELS, stride=PIECE), :]
                si = coefs[q, pl.ds(TILES + t, CHANNELS, stride=PIECE), :]
                vec = mil_use[:, at].astype(F32) * (TWO_PI / BOX_LEN)
                for d in range(4):
                    lc, ls = (co, si) if d == 0 else (vec[d - 1 : d] * si, -vec[d - 1 : d] * co)
                    for part, value in ((0, lc), (1, ls)):
                        hi, lo = split(value)
                        first = (2 * (q - 2 * h) + part) * CHUNK + t * 128
                        to = slice(first, first + 128)
                        left[d * CHANNELS : (d + 1) * CHANNELS, to] = hi
                        left[(4 + d) * CHANNELS : (5 + d) * CHANNELS, to] = lo

        span = slice(h * 2 * CHUNK, (h + 1) * 2 * CHUNK)

        def one_chip(i, carry):
            chip = lax.rem(x + 1 + i, chips)
            at = pl.ds(pl.multiple_of(chip * SLICE, SLICE), SLICE)
            both = dot(left[...], jnp.concatenate([hi_a[at, span], hi_b[at, span]], 1), NT)
            rest = dot(left[:wide, :], jnp.concatenate([lo_a[at, span], lo_b[at, span]], 1), NT)
            total = both[:wide] + both[wide:] + rest
            if h > 0:
                total = total + grads[:, at]
            if h < chunks // 2 - 1:
                grads[:, at] = total
                return carry
            weight = wbuf[:, at]
            comps = [
                jnp.sum(weight * total[CHANNELS * (d + 1) : CHANNELS * (d + 2)], 0, keepdims=True) for d in range(3)
            ]
            comps = jnp.concatenate(comps + [jnp.zeros((1, SLICE), F32)], 0)
            for c in range(2):
                g = chip * 2 + c
                gw_send[g] = total[:CHANNELS, c * beads : (c + 1) * beads]
                gp_send[g] = comps[:, c * beads : (c + 1) * beads]

                @pl.when(g != own)
                def _():
                    for copy in sum_copies(g, lax.rem(g - own + SHARERS, SHARERS)):
                        copy.start()

            return carry

        lax.fori_loop(0, chips, one_chip, 0)

    for h in range(chunks // 2):
        backward(h)

    kept = [
        pltpu.make_async_copy(gw_send.at[own], gw_recv.at[own], in_sem.at[0]),
        pltpu.make_async_copy(gp_send.at[own], gp_recv.at[own], in_sem.at[1]),
    ]
    for copy in kept:
        copy.start()
    for s in range(1, SHARERS):
        for copy in sum_copies(lax.rem(own + s, SHARERS), s):
            copy.wait_recv()
    for copy in kept:
        copy.wait()

    for s in range(1, SHARERS):
        pos_copy(s).wait_send()
        wts_copy(s).wait_send()
        for copy in sum_copies(lax.rem(own + s, SHARERS), s):
            copy.wait_send()
    for q in range(chunks):
        all_pieces(amps, q, r_send, r_recv).wait_send()
        all_pieces(coefs, q, c_send, c_recv).wait_send()

    @pl.when(core == 0)
    def _():
        mil_copy.wait_send()
        obs_copy.wait_send()


def total_kernel(gw_parts, gp_parts, gw_out, gp_out):
    gw, gp = gw_parts[0], gp_parts[0]
    for g in range(1, SHARERS):
        gw, gp = gw + gw_parts[g], gp + gp_parts[g]
    gw_out[...] = gw
    gp_out[...] = gp[:3]


def per_device(miller, lattice_pos, weights, observed):
    waves, beads = miller.shape[1], lattice_pos.shape[1]
    many = SHARERS * beads
    chunks = waves // CHUNK
    hbm = pl.BlockSpec(memory_space=pltpu.HBM)
    vmem = pl.BlockSpec(memory_space=pltpu.VMEM)
    dma = pltpu.SemaphoreType.DMA
    pieces = pltpu.VMEM((chunks, REDUCERS * PIECE, 128), F32)
    sent = [pltpu.VMEM((SHARERS, CHANNELS, beads), F32), pltpu.VMEM((SHARERS, 4, beads), F32)]
    parts = pl.pallas_call(
        kernel,
        out_shape=(
            jax.ShapeDtypeStruct((SHARERS, CHANNELS, beads), F32),
            jax.ShapeDtypeStruct((SHARERS, 4, beads), F32),
        ),
        in_specs=[hbm] * 4,
        out_specs=[hbm] * 2,
        scratch_shapes=[
            pltpu.VMEM(miller.shape, jnp.int32),
            pltpu.VMEM(miller.shape, jnp.int32),
            pltpu.VMEM(lattice_pos.shape, jnp.int32),
            pltpu.VMEM(observed.shape, F32),
            pltpu.VMEM((waves // 128, 128), F32),
            pltpu.VMEM((waves // 128, 128), F32),
            pltpu.VMEM((8, many), F32),
            pltpu.VMEM((CHANNELS, many), F32),
            pltpu.VMEM((8, waves), BF16),
            pltpu.VMEM((many, 8), BF16),
            pltpu.VMEM((2 * CHANNELS, many), BF16),
        ]
        + [pltpu.VMEM((many, waves), BF16)] * 4
        + [pltpu.VMEM((many, CHUNK), F32)]
        + [pieces] * 3
        + [pltpu.VMEM((8 * CHANNELS, 4 * CHUNK), BF16), pltpu.VMEM((4 * CHANNELS, many), F32)]
        + sent
        + [
            dma((4,)),
            dma((2, SHARERS)),
            dma((2, SHARERS)),
            dma((2,)),
            dma((2,)),
            dma((chunks,)),
            dma((chunks,)),
            dma((chunks,)),
            dma((chunks,)),
            dma((2, SHARERS)),
            dma((2, SHARERS)),
            pltpu.SemaphoreType.REGULAR,
            pltpu.SemaphoreType.REGULAR,
        ],
        compiler_params=pltpu.CompilerParams(
            collective_id=0, has_side_effects=True, vmem_limit_bytes=56 * 1024 * 1024
        ),
    )(miller, lattice_pos, weights, observed)
    return pl.pallas_call(
        total_kernel,
        out_shape=(
            jax.ShapeDtypeStruct((CHANNELS, beads), F32),
            jax.ShapeDtypeStruct((3, beads), F32),
        ),
        in_specs=[vmem] * 2,
        out_specs=[vmem] * 2,
    )(*parts)


def solution(mesh):
    in_specs = (P(None, "kv"), P(None, ("kv", "bead")), P(None, ("kv", "bead")), P(None, "kv"))
    out_specs = (P(None, ("kv", "bead")), P(None, ("kv", "bead")))
    return jax.shard_map(
        per_device, mesh=mesh, in_specs=in_specs, out_specs=out_specs, check_vma=False
    )
```

```python
import functools
import math

import jax
import jax.numpy as jnp
from jax import lax
from jax.experimental import pallas as pl
from jax.experimental.pallas import tpu as pltpu
from jax.sharding import PartitionSpec as P

CHANNELS = 32
LATTICE = 4096
BOX_LEN = 64
BEADS = 32768
TWO_PI = 2.0 * math.pi
MESH = pl.DeviceIdType.MESH
BF16 = jnp.bfloat16
F32 = jnp.float32

SIN_POLY = (4.442867755889893, -7.307443618774414, 3.594788074493408, -0.784373939037323)
COS_POLY = (1.4142135381698608, -6.978850841522217, 5.7394609451293945, -1.8835629224777222, 0.31069815158843994)

SHARERS = 8
REDUCERS = 32
CHUNKS = (256, 256, 256, 256)
STARTS = tuple(sum(CHUNKS[:q]) for q in range(len(CHUNKS)))
BASES = tuple(2 * sum(CHUNKS[q % 2 : q : 2]) for q in range(len(CHUNKS)))
GROUPS = ((0, 1), (2, 3))
SLICE = 256
PIECES = tuple(2 * size // 128 for size in CHUNKS)
NT = (((1,), (1,)), ((), ()))
NN = (((1,), (0,)), ((), ()))


FAR_FIRST = sorted(
    ((dy, dz) for dy in range(4) for dz in range(8) if dy or dz),
    key=lambda step: -min(step[0], 4 - step[0]) - min(step[1], 8 - step[1]),
)


def poly(u, coefs):
    total = u * coefs[-1] + coefs[-2]
    for c in coefs[-3::-1]:
        total = total * u + c
    return total


def cos_sin(turns):
    f = turns - jnp.round(turns)
    u = f * f
    s = poly(u, SIN_POLY) * f
    c = poly(u, COS_POLY)
    return 1.0 - s * s, s * c


def split(x):
    high = x.astype(BF16)
    return high, (x - high.astype(F32)).astype(BF16)


def dot(a, b, dims):
    return lax.dot_general(a, b, dims, preferred_element_type=F32)


def kernel(
    mil, pos, wts, obs, gw_recv, gp_recv,
    mil_own, mil_use, pos_own, obs_own, obs_row, obs_send, posbuf, wbuf, mil_rows, pos_t, wsplit,
    hi_a, lo_a, hi_b, lo_b, phase,
    amps, shares, coefs, left, grads, gw_send, gp_send,
    in_sem, a_send, a_recv, m_send, m_recv, r_send, r_recv, c_send, c_recv, d_send, d_recv,
    ready, met,
):
    kv, bead = lax.axis_index("kv"), lax.axis_index("bead")
    z_low, x = kv // 4, lax.rem(kv, 4)
    core = lax.rem(bead, 2)
    own = x * 2 + core
    channel = (bead // 8) * 8 + lax.rem(bead // 2, 4) * 2 + z_low
    waves, beads = mil_use.shape[1], pos.shape[1]
    chunks = len(CHUNKS)
    chips = SHARERS // 2

    def sharer(g):
        return (z_low * 4 + g // 2, (bead // 2) * 2 + lax.rem(g, 2))

    def reducer(r, to_core):
        y, z = r // 8, lax.rem(r, 8)
        return (lax.rem(z, 2) * 4 + x, (y * 4 + z // 2) * 2 + to_core)

    def others():
        for dy, dz in FAR_FIRST:
            yield lax.rem(channel // 8 + dy, 4) * 8 + lax.rem(channel + dz, 8)

    def remote(src, dst, send, recv, device):
        return pltpu.make_async_remote_copy(
            src_ref=src, dst_ref=dst, send_sem=send, recv_sem=recv, device_id=device, device_id_type=MESH
        )

    def greet(device):
        pl.semaphore_signal(barrier, inc=1, device_id=device, device_id_type=MESH)

    def lanes(g):
        return pl.ds(pl.multiple_of(g * beads, beads), beads)

    barrier = pltpu.get_barrier_semaphore()
    for s in range(1, chips):
        greet(sharer(2 * lax.rem(x + s, chips)))

    @pl.when(core == 1)
    def _():
        greet((kv, bead - 1))

    greet(((1 - z_low) * 4 + x, bead - core))
    inputs = [
        pltpu.make_async_copy(src, dst, in_sem.at[i])
        for i, (src, dst) in enumerate(
            ((pos, pos_own), (wts, wbuf.at[:, lanes(own)]), (mil, mil_own), (obs, obs_own))
        )
    ]
    for copy in inputs:
        copy.start()
    for s in range(1, REDUCERS):
        greet(reducer(lax.rem(channel + s, REDUCERS), 1))
    for copy in inputs:
        copy.wait()

    where = pos_own[...].astype(F32)
    upper = jnp.floor(where * (1.0 / 64.0))
    lower = where - 64.0 * upper
    posbuf[:, lanes(own)] = jnp.concatenate(
        [upper * (1.0 / 64.0), lower * (1.0 / LATTICE), jnp.zeros((2, beads), F32)], 0
    )

    def put_row(ref, row):
        for t in range(waves // 128):
            ref[t : t + 1, :] = row[:, t * 128 : (t + 1) * 128]

    @pl.when(core == 0)
    def _():
        put_row(obs_send, obs_own[pl.ds(channel + 1 - 2 * z_low, 1), :])

    @pl.when(core == z_low)
    def _():
        mil_use[...] = mil_own[...]
        put_row(obs_row, obs_own[pl.ds(channel, 1), :])

    @pl.when(core == 0)
    def _():
        pl.semaphore_wait(barrier, SHARERS - 1 + 2)
        pl.semaphore_signal(ready, inc=1, device_id=(kv, bead + 1), device_id_type=MESH)

    @pl.when(core == 1)
    def _():
        pl.semaphore_wait(ready, 1)

    def pos_copy(s):
        g = lax.rem(own + s, SHARERS)
        at = posbuf.at[:, lanes(own)]
        return remote(at, at, a_send.at[0, s], a_recv.at[0, s], sharer(g))

    def wts_copy(s):
        g = lax.rem(own + s, SHARERS)
        at = wbuf.at[:, lanes(own)]
        return remote(at, at, a_send.at[1, s], a_recv.at[1, s], sharer(g))

    beyond = ((1 - z_low) * 4 + x, bead - core + z_low)
    mil_copy = remote(mil_own, mil_use, m_send.at[0], m_recv.at[0], beyond)
    obs_copy = remote(obs_send, obs_row, m_send.at[1], m_recv.at[1], beyond)

    for s in range(1, SHARERS):
        pos_copy(s).start()

    @pl.when(core == 0)
    def _():
        mil_copy.start()
        obs_copy.start()

    for s in range(1, SHARERS):
        wts_copy(s).start()

    @pl.when(core != z_low)
    def _():
        mil_copy.wait_recv()

    index = mil_use[...].astype(F32)
    mil_rows[...] = jnp.concatenate([index, index, jnp.zeros((2, waves), F32)], 0).astype(BF16)

    sets = ((hi_a, lo_a), (hi_b, lo_b))
    rows = 32

    def piece_rows(q, r):
        return pl.ds(pl.multiple_of(r * PIECES[q], PIECES[q]), PIECES[q])

    def share_copy(q, to):
        src, dst = amps.at[q, piece_rows(q, to), :], shares.at[q, piece_rows(q, channel), :]
        return remote(src, dst, r_send.at[q], r_recv.at[q], reducer(to, core))

    def coef_copy(q, to):
        at = coefs.at[q, piece_rows(q, channel), :]
        return remote(at, at, c_send.at[q], c_recv.at[q], reducer(to, core))

    def all_pieces(buf, q, send, recv):
        at = buf.at[q, pl.ds(0, (REDUCERS - 1) * PIECES[q]), :]
        return remote(at, at, send.at[q], recv.at[q], reducer(lax.rem(channel + 1, REDUCERS), core))

    def add(q):
        hi, lo = sets[q % 2]
        at = slice(BASES[q], BASES[q] + 2 * CHUNKS[q])
        both = dot(wsplit[...], hi[:, at], NN)
        amp = both[:CHANNELS] + both[CHANNELS:] + dot(wsplit[:CHANNELS, :], lo[:, at], NN)
        for t in range(PIECES[q]):
            amps[q, pl.ds(t, REDUCERS, stride=PIECES[q]), :] = amp[:, t * 128 : (t + 1) * 128]

    def make(q, first=0, count=SHARERS * beads):
        (hi, lo), size = sets[q % 2], CHUNKS[q]
        phase[0:count, 0:size] = dot(
            pos_t[pl.ds(first, count), :], mil_rows[:, STARTS[q] : STARTS[q] + size], NN
        )
        for r in range(0, count, rows):
            to = pl.ds(first + r, rows) if isinstance(first, int) else pl.ds(pl.multiple_of(first + r, rows), rows)
            for part, value in enumerate(cos_sin(phase[r : r + rows, 0:size])):
                at = slice(BASES[q] + part * size, BASES[q] + (part + 1) * size)
                hi[to, at], lo[to, at] = split(value)

    def send_shares(q):
        for r in others():
            share_copy(q, r).start()
        shares[q, piece_rows(q, channel), :] = amps[q, piece_rows(q, channel), :]

    for step in (0, 1, 3, 2):
        chip = lax.rem(x + step, chips)
        for c in range(2):
            g = chip * 2 + c
            shift = lax.rem(own - g + SHARERS, SHARERS)
            if step:
                pos_copy(shift).wait_recv()
            else:

                @pl.when(g != own)
                def _():
                    pos_copy(shift).wait_recv()

        here = pl.multiple_of(chip * SLICE, SLICE)
        pos_t[pl.ds(here, SLICE), :] = posbuf[:, pl.ds(here, SLICE)].T.astype(BF16)
        for q in range(1 if step else chunks):
            make(q, here, SLICE)

    for s in range(1, SHARERS):
        wts_copy(s).wait_recv()
    high, low = split(wbuf[...])
    wsplit[...] = jnp.concatenate([high, low], 0)

    for q in range(chunks):
        add(q)
        if q + 1 < chunks:
            for step in (1, 3, 2):
                make(q + 1, pl.multiple_of(lax.rem(x + step, chips) * SLICE, SLICE), SLICE)
        if q == 0:

            @pl.when(core == 1)
            def _():
                pl.semaphore_wait(barrier, 2 * (REDUCERS - 1))
                pl.semaphore_signal(met, inc=1, device_id=(kv, bead - 1), device_id_type=MESH)

            @pl.when(core == 0)
            def _():
                pl.semaphore_wait(met, 1)

        send_shares(q)

    @pl.when(core != z_low)
    def _():
        obs_copy.wait_recv()

    bead_total = float(BEADS)

    for q in range(chunks):
        all_pieces(shares, q, r_send, r_recv).wait_recv()
        rows_in, tiles = PIECES[q], CHUNKS[q] // 128
        total = shares[q, 0:8, :]
        for r in range(8, REDUCERS * rows_in, 8):
            total = total + shares[q, r : r + 8, :]
        total = sum(total[r : r + rows_in] for r in range(0, 8, rows_in))
        amp_cos, amp_sin = total[:tiles], total[tiles:]
        measured = obs_row[STARTS[q] // 128 : STARTS[q] // 128 + tiles, :]
        residual = (amp_cos * amp_cos + amp_sin * amp_sin) * (1.0 / bead_total) - measured
        scale = residual * (2.0 / bead_total)
        coefs[q, piece_rows(q, channel), :] = jnp.concatenate([scale * amp_cos, scale * amp_sin], 0)
        for r in others():
            coef_copy(q, r).start()

    wide = 4 * CHANNELS

    def sum_copies(g, s):
        device = sharer(g)
        return (
            remote(gw_send.at[g], gw_recv.at[own], d_send.at[0, s], d_recv.at[0, s], device),
            remote(gp_send.at[g], gp_recv.at[own], d_send.at[1, s], d_recv.at[1, s], device),
        )

    def backward(group):
        filled = 0
        for q in group:
            all_pieces(coefs, q, c_send, c_recv).wait_recv()
            tiles = CHUNKS[q] // 128
            for t in range(tiles):
                at = slice(STARTS[q] + t * 128, STARTS[q] + (t + 1) * 128)
                co = coefs[q, pl.ds(t, CHANNELS, stride=PIECES[q]), :]
                si = coefs[q, pl.ds(tiles + t, CHANNELS, stride=PIECES[q]), :]
                vec = mil_use[:, at].astype(F32) * (TWO_PI / BOX_LEN)
                for d in range(4):
                    lc, ls = (co, si) if d == 0 else (vec[d - 1 : d] * si, -vec[d - 1 : d] * co)
                    for part, value in ((0, lc), (1, ls)):
                        hi, lo = split(value)
                        first = filled + part * CHUNKS[q] + t * 128
                        to = slice(first, first + 128)
                        left[d * CHANNELS : (d + 1) * CHANNELS, to] = hi
                        left[(4 + d) * CHANNELS : (5 + d) * CHANNELS, to] = lo
            filled += 2 * CHUNKS[q]

        def held(part, at):
            return jnp.concatenate(
                [sets[q % 2][part][at, BASES[q] : BASES[q] + 2 * CHUNKS[q]] for q in group], 1
            )

        def one_chip(i, carry):
            chip = lax.rem(x + 1 + i, chips)
            at = pl.ds(pl.multiple_of(chip * SLICE, SLICE), SLICE)
            both = dot(left[:, :filled], held(0, at), NT)
            rest = dot(left[:wide, :filled], held(1, at), NT)
            total = both[:wide] + both[wide:] + rest
            if group[0] > 0:
                total = total + grads[:, at]
            if group[-1] < chunks - 1:
                grads[:, at] = total
                return carry
            weight = wbuf[:, at]
            comps = [
                jnp.sum(weight * total[CHANNELS * (d + 1) : CHANNELS * (d + 2)], 0, keepdims=True) for d in range(3)
            ]
            comps = jnp.concatenate(comps + [jnp.zeros((1, SLICE), F32)], 0)
            for c in range(2):
                g = chip * 2 + c
                gw_send[g] = total[:CHANNELS, c * beads : (c + 1) * beads]
                gp_send[g] = comps[:, c * beads : (c + 1) * beads]

                @pl.when(g != own)
                def _():
                    for copy in sum_copies(g, lax.rem(g - own + SHARERS, SHARERS)):
                        copy.start()

            return carry

        lax.fori_loop(0, chips, one_chip, 0)

    for group in GROUPS:
        backward(group)

    kept = [
        pltpu.make_async_copy(gw_send.at[own], gw_recv.at[own], in_sem.at[0]),
        pltpu.make_async_copy(gp_send.at[own], gp_recv.at[own], in_sem.at[1]),
    ]
    for copy in kept:
        copy.start()
    for s in range(1, SHARERS):
        for copy in sum_copies(lax.rem(own + s, SHARERS), s):
            copy.wait_recv()
    for copy in kept:
        copy.wait()

    for s in range(1, SHARERS):
        pos_copy(s).wait_send()
        wts_copy(s).wait_send()
        for copy in sum_copies(lax.rem(own + s, SHARERS), s):
            copy.wait_send()
    for q in range(chunks):
        all_pieces(amps, q, r_send, r_recv).wait_send()
        all_pieces(coefs, q, c_send, c_recv).wait_send()

    @pl.when(core == 0)
    def _():
        mil_copy.wait_send()
        obs_copy.wait_send()


def total_kernel(gw_parts, gp_parts, gw_out, gp_out):
    gw, gp = gw_parts[0], gp_parts[0]
    for g in range(1, SHARERS):
        gw, gp = gw + gw_parts[g], gp + gp_parts[g]
    gw_out[...] = gw
    gp_out[...] = gp[:3]


def per_device(miller, lattice_pos, weights, observed):
    waves, beads = miller.shape[1], lattice_pos.shape[1]
    many = SHARERS * beads
    chunks = len(CHUNKS)
    assert sum(CHUNKS) == waves
    hbm = pl.BlockSpec(memory_space=pltpu.HBM)
    vmem = pl.BlockSpec(memory_space=pltpu.VMEM)
    dma = pltpu.SemaphoreType.DMA
    pieces = pltpu.VMEM((chunks, REDUCERS * max(PIECES), 128), F32)
    sent = [pltpu.VMEM((SHARERS, CHANNELS, beads), F32), pltpu.VMEM((SHARERS, 4, beads), F32)]
    parts = pl.pallas_call(
        kernel,
        out_shape=(
            jax.ShapeDtypeStruct((SHARERS, CHANNELS, beads), F32),
            jax.ShapeDtypeStruct((SHARERS, 4, beads), F32),
        ),
        in_specs=[hbm] * 4,
        out_specs=[hbm] * 2,
        scratch_shapes=[
            pltpu.VMEM(miller.shape, jnp.int32),
            pltpu.VMEM(miller.shape, jnp.int32),
            pltpu.VMEM(lattice_pos.shape, jnp.int32),
            pltpu.VMEM(observed.shape, F32),
            pltpu.VMEM((waves // 128, 128), F32),
            pltpu.VMEM((waves // 128, 128), F32),
            pltpu.VMEM((8, many), F32),
            pltpu.VMEM((CHANNELS, many), F32),
            pltpu.VMEM((8, waves), BF16),
            pltpu.VMEM((many, 8), BF16),
            pltpu.VMEM((2 * CHANNELS, many), BF16),
        ]
        + [pltpu.VMEM((many, 2 * sum(CHUNKS[turn::2])), BF16) for turn in (0, 0, 1, 1)]
        + [pltpu.VMEM((many, max(CHUNKS)), F32)]
        + [pieces] * 3
        + [pltpu.VMEM((8 * CHANNELS, max(2 * sum(CHUNKS[q] for q in group) for group in GROUPS)), BF16), pltpu.VMEM((4 * CHANNELS, many), F32)]
        + sent
        + [
            dma((4,)),
            dma((2, SHARERS)),
            dma((2, SHARERS)),
            dma((2,)),
            dma((2,)),
            dma((chunks,)),
            dma((chunks,)),
            dma((chunks,)),
            dma((chunks,)),
            dma((2, SHARERS)),
            dma((2, SHARERS)),
            pltpu.SemaphoreType.REGULAR,
            pltpu.SemaphoreType.REGULAR,
        ],
        compiler_params=pltpu.CompilerParams(
            collective_id=0, has_side_effects=True, vmem_limit_bytes=56 * 1024 * 1024
        ),
    )(miller, lattice_pos, weights, observed)
    return pl.pallas_call(
        total_kernel,
        out_shape=(
            jax.ShapeDtypeStruct((CHANNELS, beads), F32),
            jax.ShapeDtypeStruct((3, beads), F32),
        ),
        in_specs=[vmem] * 2,
        out_specs=[vmem] * 2,
    )(*parts)


def solution(mesh):
    in_specs = (P(None, "kv"), P(None, ("kv", "bead")), P(None, ("kv", "bead")), P(None, "kv"))
    out_specs = (P(None, ("kv", "bead")), P(None, ("kv", "bead")))
    return jax.shard_map(
        per_device, mesh=mesh, in_specs=in_specs, out_specs=out_specs, check_vma=False
    )
```

```python
import functools
import math

import jax
import jax.numpy as jnp
from jax import lax
from jax.experimental import pallas as pl
from jax.experimental.pallas import tpu as pltpu
from jax.sharding import PartitionSpec as P

CHANNELS = 32
LATTICE = 4096
BOX_LEN = 64
BEADS = 32768
TWO_PI = 2.0 * math.pi
MESH = pl.DeviceIdType.MESH
BF16 = jnp.bfloat16
F32 = jnp.float32

SIN_POLY = (2.641753911972046, -1.0863758325576782, 0.13399836421012878, -0.0077232783660292625)

SHARERS = 8
REDUCERS = 32
CHUNKS = (256, 256, 256, 256)
STARTS = tuple(sum(CHUNKS[:q]) for q in range(len(CHUNKS)))
BASES = tuple(2 * sum(CHUNKS[q % 2 : q : 2]) for q in range(len(CHUNKS)))
GROUPS = ((0, 1), (2, 3))
SLICE = 256
PIECES = tuple(2 * size // 128 for size in CHUNKS)
NT = (((1,), (1,)), ((), ()))
NN = (((1,), (0,)), ((), ()))


FAR_FIRST = sorted(
    ((dy, dz) for dy in range(4) for dz in range(8) if dy or dz),
    key=lambda step: -min(step[0], 4 - step[0]) - min(step[1], 8 - step[1]),
)


def poly(u, coefs):
    total = u * coefs[-1] + coefs[-2]
    for c in coefs[-3::-1]:
        total = total * u + c
    return total


def cos_sin(turns):
    f = turns - jnp.round(turns)
    quarter = poly(f * f, SIN_POLY) * f
    square = quarter * quarter
    rest = 2.0 * math.sqrt(2.0) - square
    half_sin = quarter * (rest * lax.rsqrt(rest))
    half_cos = math.sqrt(2.0) - square
    return 1.0 - half_sin * half_sin, half_sin * half_cos


def split(x):
    high = x.astype(BF16)
    return high, (x - high.astype(F32)).astype(BF16)


def dot(a, b, dims):
    return lax.dot_general(a, b, dims, preferred_element_type=F32)


def kernel(
    mil, pos, wts, obs, gw_recv, gp_recv,
    mil_own, mil_use, pos_own, obs_own, obs_row, obs_send, posbuf, wbuf, mil_rows, pos_t, wsplit,
    hi_a, lo_a, hi_b, lo_b, phase,
    amps, shares, coefs, left, grads, gw_send, gp_send,
    in_sem, a_send, a_recv, m_send, m_recv, r_send, r_recv, c_send, c_recv, d_send, d_recv,
    ready, met,
):
    kv, bead = lax.axis_index("kv"), lax.axis_index("bead")
    z_low, x = kv // 4, lax.rem(kv, 4)
    core = lax.rem(bead, 2)
    own = x * 2 + core
    channel = (bead // 8) * 8 + lax.rem(bead // 2, 4) * 2 + z_low
    waves, beads = mil_use.shape[1], pos.shape[1]
    chunks = len(CHUNKS)
    chips = SHARERS // 2

    def sharer(g):
        return (z_low * 4 + g // 2, (bead // 2) * 2 + lax.rem(g, 2))

    def reducer(r, to_core):
        y, z = r // 8, lax.rem(r, 8)
        return (lax.rem(z, 2) * 4 + x, (y * 4 + z // 2) * 2 + to_core)

    def others():
        for dy, dz in FAR_FIRST:
            yield lax.rem(channel // 8 + dy, 4) * 8 + lax.rem(channel + dz, 8)

    def remote(src, dst, send, recv, device):
        return pltpu.make_async_remote_copy(
            src_ref=src, dst_ref=dst, send_sem=send, recv_sem=recv, device_id=device, device_id_type=MESH
        )

    def greet(device):
        pl.semaphore_signal(barrier, inc=1, device_id=device, device_id_type=MESH)

    def lanes(g):
        return pl.ds(pl.multiple_of(g * beads, beads), beads)

    barrier = pltpu.get_barrier_semaphore()
    for s in range(1, chips):
        greet(sharer(2 * lax.rem(x + s, chips)))

    @pl.when(core == 1)
    def _():
        greet((kv, bead - 1))

    greet(((1 - z_low) * 4 + x, bead - core))
    inputs = [
        pltpu.make_async_copy(src, dst, in_sem.at[i])
        for i, (src, dst) in enumerate(
            ((pos, pos_own), (wts, wbuf.at[:, lanes(own)]), (mil, mil_own), (obs, obs_own))
        )
    ]
    for copy in inputs:
        copy.start()
    for s in range(1, REDUCERS):
        greet(reducer(lax.rem(channel + s, REDUCERS), 1))
    for copy in inputs:
        copy.wait()

    where = pos_own[...].astype(F32)
    upper = jnp.floor(where * (1.0 / 64.0))
    lower = where - 64.0 * upper
    posbuf[:, lanes(own)] = jnp.concatenate(
        [upper * (1.0 / 64.0), lower * (1.0 / LATTICE), jnp.zeros((2, beads), F32)], 0
    )

    def put_row(ref, row):
        for t in range(waves // 128):
            ref[t : t + 1, :] = row[:, t * 128 : (t + 1) * 128]

    @pl.when(core == 0)
    def _():
        put_row(obs_send, obs_own[pl.ds(channel + 1 - 2 * z_low, 1), :])

    @pl.when(core == z_low)
    def _():
        mil_use[...] = mil_own[...]
        put_row(obs_row, obs_own[pl.ds(channel, 1), :])

    @pl.when(core == 0)
    def _():
        pl.semaphore_wait(barrier, SHARERS - 1 + 2)
        pl.semaphore_signal(ready, inc=1, device_id=(kv, bead + 1), device_id_type=MESH)

    @pl.when(core == 1)
    def _():
        pl.semaphore_wait(ready, 1)

    def pos_copy(s):
        g = lax.rem(own + s, SHARERS)
        at = posbuf.at[:, lanes(own)]
        return remote(at, at, a_send.at[0, s], a_recv.at[0, s], sharer(g))

    def wts_copy(s):
        g = lax.rem(own + s, SHARERS)
        at = wbuf.at[:, lanes(own)]
        return remote(at, at, a_send.at[1, s], a_recv.at[1, s], sharer(g))

    beyond = ((1 - z_low) * 4 + x, bead - core + z_low)
    mil_copy = remote(mil_own, mil_use, m_send.at[0], m_recv.at[0], beyond)
    obs_copy = remote(obs_send, obs_row, m_send.at[1], m_recv.at[1], beyond)

    for s in range(1, SHARERS):
        pos_copy(s).start()

    @pl.when(core == 0)
    def _():
        mil_copy.start()
        obs_copy.start()

    for s in range(1, SHARERS):
        wts_copy(s).start()

    @pl.when(core != z_low)
    def _():
        mil_copy.wait_recv()

    index = mil_use[...].astype(F32)
    mil_rows[...] = jnp.concatenate([index, index, jnp.zeros((2, waves), F32)], 0).astype(BF16)

    sets = ((hi_a, lo_a), (hi_b, lo_b))
    rows = 32

    def piece_rows(q, r):
        return pl.ds(pl.multiple_of(r * PIECES[q], PIECES[q]), PIECES[q])

    def share_copy(q, to):
        src, dst = amps.at[q, piece_rows(q, to), :], shares.at[q, piece_rows(q, channel), :]
        return remote(src, dst, r_send.at[q], r_recv.at[q], reducer(to, core))

    def coef_copy(q, to):
        at = coefs.at[q, piece_rows(q, channel), :]
        return remote(at, at, c_send.at[q], c_recv.at[q], reducer(to, core))

    def all_pieces(buf, q, send, recv):
        at = buf.at[q, pl.ds(0, (REDUCERS - 1) * PIECES[q]), :]
        return remote(at, at, send.at[q], recv.at[q], reducer(lax.rem(channel + 1, REDUCERS), core))

    def add(q):
        hi, lo = sets[q % 2]
        at = slice(BASES[q], BASES[q] + 2 * CHUNKS[q])
        both = dot(wsplit[...], hi[:, at], NN)
        amp = both[:CHANNELS] + both[CHANNELS:] + dot(wsplit[:CHANNELS, :], lo[:, at], NN)
        for t in range(PIECES[q]):
            amps[q, pl.ds(t, REDUCERS, stride=PIECES[q]), :] = amp[:, t * 128 : (t + 1) * 128]

    def make(q, first=0, count=SHARERS * beads):
        (hi, lo), size = sets[q % 2], CHUNKS[q]
        phase[0:count, 0:size] = dot(
            pos_t[pl.ds(first, count), :], mil_rows[:, STARTS[q] : STARTS[q] + size], NN
        )
        for r in range(0, count, rows):
            to = pl.ds(first + r, rows) if isinstance(first, int) else pl.ds(pl.multiple_of(first + r, rows), rows)
            for part, value in enumerate(cos_sin(phase[r : r + rows, 0:size])):
                at = slice(BASES[q] + part * size, BASES[q] + (part + 1) * size)
                hi[to, at], lo[to, at] = split(value)

    def send_shares(q):
        for r in others():
            share_copy(q, r).start()
        shares[q, piece_rows(q, channel), :] = amps[q, piece_rows(q, channel), :]

    for step in (0, 1, 3, 2):
        chip = lax.rem(x + step, chips)
        for c in range(2):
            g = chip * 2 + c
            shift = lax.rem(own - g + SHARERS, SHARERS)
            if step:
                pos_copy(shift).wait_recv()
            else:

                @pl.when(g != own)
                def _():
                    pos_copy(shift).wait_recv()

        here = pl.multiple_of(chip * SLICE, SLICE)
        pos_t[pl.ds(here, SLICE), :] = posbuf[:, pl.ds(here, SLICE)].T.astype(BF16)
        for q in range(1 if step else chunks):
            make(q, here, SLICE)

    for s in range(1, SHARERS):
        wts_copy(s).wait_recv()
    high, low = split(wbuf[...])
    wsplit[...] = jnp.concatenate([high, low], 0)

    for q in range(chunks):
        add(q)
        if q + 1 < chunks:
            for step in (1, 3, 2):
                make(q + 1, pl.multiple_of(lax.rem(x + step, chips) * SLICE, SLICE), SLICE)
        if q == 0:

            @pl.when(core == 1)
            def _():
                pl.semaphore_wait(barrier, 2 * (REDUCERS - 1))
                pl.semaphore_signal(met, inc=1, device_id=(kv, bead - 1), device_id_type=MESH)

            @pl.when(core == 0)
            def _():
                pl.semaphore_wait(met, 1)

        send_shares(q)

    @pl.when(core != z_low)
    def _():
        obs_copy.wait_recv()

    bead_total = float(BEADS)

    for q in range(chunks):
        all_pieces(shares, q, r_send, r_recv).wait_recv()
        rows_in, tiles = PIECES[q], CHUNKS[q] // 128
        total = shares[q, 0:8, :]
        for r in range(8, REDUCERS * rows_in, 8):
            total = total + shares[q, r : r + 8, :]
        total = sum(total[r : r + rows_in] for r in range(0, 8, rows_in))
        amp_cos, amp_sin = total[:tiles], total[tiles:]
        measured = obs_row[STARTS[q] // 128 : STARTS[q] // 128 + tiles, :]
        residual = (amp_cos * amp_cos + amp_sin * amp_sin) * (1.0 / bead_total) - measured
        scale = residual * (2.0 / bead_total)
        coefs[q, piece_rows(q, channel), :] = jnp.concatenate([scale * amp_cos, scale * amp_sin], 0)
        for r in others():
            coef_copy(q, r).start()

    wide = 4 * CHANNELS

    def sum_copies(g, s):
        device = sharer(g)
        return (
            remote(gw_send.at[g], gw_recv.at[own], d_send.at[0, s], d_recv.at[0, s], device),
            remote(gp_send.at[g], gp_recv.at[own], d_send.at[1, s], d_recv.at[1, s], device),
        )

    def backward(group):
        filled = 0
        for q in group:
            all_pieces(coefs, q, c_send, c_recv).wait_recv()
            tiles = CHUNKS[q] // 128
            for t in range(tiles):
                at = slice(STARTS[q] + t * 128, STARTS[q] + (t + 1) * 128)
                co = coefs[q, pl.ds(t, CHANNELS, stride=PIECES[q]), :]
                si = coefs[q, pl.ds(tiles + t, CHANNELS, stride=PIECES[q]), :]
                vec = mil_use[:, at].astype(F32) * (TWO_PI / BOX_LEN)
                for d in range(4):
                    lc, ls = (co, si) if d == 0 else (vec[d - 1 : d] * si, -vec[d - 1 : d] * co)
                    for part, value in ((0, lc), (1, ls)):
                        hi, lo = split(value)
                        first = filled + part * CHUNKS[q] + t * 128
                        to = slice(first, first + 128)
                        left[d * CHANNELS : (d + 1) * CHANNELS, to] = hi
                        left[(4 + d) * CHANNELS : (5 + d) * CHANNELS, to] = lo
            filled += 2 * CHUNKS[q]

        def held(part, at):
            return jnp.concatenate(
                [sets[q % 2][part][at, BASES[q] : BASES[q] + 2 * CHUNKS[q]] for q in group], 1
            )

        def one_chip(i, carry):
            chip = lax.rem(x + 1 + i, chips)
            at = pl.ds(pl.multiple_of(chip * SLICE, SLICE), SLICE)
            both = dot(left[:, :filled], held(0, at), NT)
            rest = dot(left[:wide, :filled], held(1, at), NT)
            total = both[:wide] + both[wide:] + rest
            if group[0] > 0:
                total = total + grads[:, at]
            if group[-1] < chunks - 1:
                grads[:, at] = total
                return carry
            weight = wbuf[:, at]
            comps = [
                jnp.sum(weight * total[CHANNELS * (d + 1) : CHANNELS * (d + 2)], 0, keepdims=True) for d in range(3)
            ]
            comps = jnp.concatenate(comps + [jnp.zeros((1, SLICE), F32)], 0)
            for c in range(2):
                g = chip * 2 + c
                gw_send[g] = total[:CHANNELS, c * beads : (c + 1) * beads]
                gp_send[g] = comps[:, c * beads : (c + 1) * beads]

                @pl.when(g != own)
                def _():
                    for copy in sum_copies(g, lax.rem(g - own + SHARERS, SHARERS)):
                        copy.start()

            return carry

        lax.fori_loop(0, chips, one_chip, 0)

    for group in GROUPS:
        backward(group)

    kept = [
        pltpu.make_async_copy(gw_send.at[own], gw_recv.at[own], in_sem.at[0]),
        pltpu.make_async_copy(gp_send.at[own], gp_recv.at[own], in_sem.at[1]),
    ]
    for copy in kept:
        copy.start()
    for s in range(1, SHARERS):
        for copy in sum_copies(lax.rem(own + s, SHARERS), s):
            copy.wait_recv()
    for copy in kept:
        copy.wait()

    for s in range(1, SHARERS):
        pos_copy(s).wait_send()
        wts_copy(s).wait_send()
        for copy in sum_copies(lax.rem(own + s, SHARERS), s):
            copy.wait_send()
    for q in range(chunks):
        all_pieces(amps, q, r_send, r_recv).wait_send()
        all_pieces(coefs, q, c_send, c_recv).wait_send()

    @pl.when(core == 0)
    def _():
        mil_copy.wait_send()
        obs_copy.wait_send()


def total_kernel(gw_parts, gp_parts, gw_out, gp_out):
    gw, gp = gw_parts[0], gp_parts[0]
    for g in range(1, SHARERS):
        gw, gp = gw + gw_parts[g], gp + gp_parts[g]
    gw_out[...] = gw
    gp_out[...] = gp[:3]


def per_device(miller, lattice_pos, weights, observed):
    waves, beads = miller.shape[1], lattice_pos.shape[1]
    many = SHARERS * beads
    chunks = len(CHUNKS)
    assert sum(CHUNKS) == waves
    hbm = pl.BlockSpec(memory_space=pltpu.HBM)
    vmem = pl.BlockSpec(memory_space=pltpu.VMEM)
    dma = pltpu.SemaphoreType.DMA
    pieces = pltpu.VMEM((chunks, REDUCERS * max(PIECES), 128), F32)
    sent = [pltpu.VMEM((SHARERS, CHANNELS, beads), F32), pltpu.VMEM((SHARERS, 4, beads), F32)]
    parts = pl.pallas_call(
        kernel,
        out_shape=(
            jax.ShapeDtypeStruct((SHARERS, CHANNELS, beads), F32),
            jax.ShapeDtypeStruct((SHARERS, 4, beads), F32),
        ),
        in_specs=[hbm] * 4,
        out_specs=[hbm] * 2,
        scratch_shapes=[
            pltpu.VMEM(miller.shape, jnp.int32),
            pltpu.VMEM(miller.shape, jnp.int32),
            pltpu.VMEM(lattice_pos.shape, jnp.int32),
            pltpu.VMEM(observed.shape, F32),
            pltpu.VMEM((waves // 128, 128), F32),
            pltpu.VMEM((waves // 128, 128), F32),
            pltpu.VMEM((8, many), F32),
            pltpu.VMEM((CHANNELS, many), F32),
            pltpu.VMEM((8, waves), BF16),
            pltpu.VMEM((many, 8), BF16),
            pltpu.VMEM((2 * CHANNELS, many), BF16),
        ]
        + [pltpu.VMEM((many, 2 * sum(CHUNKS[turn::2])), BF16) for turn in (0, 0, 1, 1)]
        + [pltpu.VMEM((many, max(CHUNKS)), F32)]
        + [pieces] * 3
        + [pltpu.VMEM((8 * CHANNELS, max(2 * sum(CHUNKS[q] for q in group) for group in GROUPS)), BF16), pltpu.VMEM((4 * CHANNELS, many), F32)]
        + sent
        + [
            dma((4,)),
            dma((2, SHARERS)),
            dma((2, SHARERS)),
            dma((2,)),
            dma((2,)),
            dma((chunks,)),
            dma((chunks,)),
            dma((chunks,)),
            dma((chunks,)),
            dma((2, SHARERS)),
            dma((2, SHARERS)),
            pltpu.SemaphoreType.REGULAR,
            pltpu.SemaphoreType.REGULAR,
        ],
        compiler_params=pltpu.CompilerParams(
            collective_id=0, has_side_effects=True, vmem_limit_bytes=56 * 1024 * 1024
        ),
    )(miller, lattice_pos, weights, observed)
    return pl.pallas_call(
        total_kernel,
        out_shape=(
            jax.ShapeDtypeStruct((CHANNELS, beads), F32),
            jax.ShapeDtypeStruct((3, beads), F32),
        ),
        in_specs=[vmem] * 2,
        out_specs=[vmem] * 2,
    )(*parts)


def solution(mesh):
    in_specs = (P(None, "kv"), P(None, ("kv", "bead")), P(None, ("kv", "bead")), P(None, "kv"))
    out_specs = (P(None, ("kv", "bead")), P(None, ("kv", "bead")))
    return jax.shard_map(
        per_device, mesh=mesh, in_specs=in_specs, out_specs=out_specs, check_vma=False
    )
```

```python
import functools
import math

import jax
import jax.numpy as jnp
from jax import lax
from jax.experimental import pallas as pl
from jax.experimental.pallas import tpu as pltpu
from jax.sharding import PartitionSpec as P

CHANNELS = 32
LATTICE = 4096
BOX_LEN = 64
BEADS = 32768
TWO_PI = 2.0 * math.pi
MESH = pl.DeviceIdType.MESH
BF16 = jnp.bfloat16
F32 = jnp.float32

SIN_POLY = (2.641753911972046, -1.0863758325576782, 0.13399836421012878, -0.0077232783660292625)

SHARERS = 8
REDUCERS = 32
CHUNK = 256
SLICE = 256
TILES = CHUNK // 128
PIECE = 2 * TILES
NT = (((1,), (1,)), ((), ()))
NN = (((1,), (0,)), ((), ()))


FAR_FIRST = sorted(
    ((dy, dz) for dy in range(4) for dz in range(8) if dy or dz),
    key=lambda step: -min(step[0], 4 - step[0]) - min(step[1], 8 - step[1]),
)


def poly(u, coefs):
    total = u * coefs[-1] + coefs[-2]
    for c in coefs[-3::-1]:
        total = total * u + c
    return total


def cos_sin(turns):
    f = turns - jnp.round(turns)
    quarter = poly(f * f, SIN_POLY) * f
    square = quarter * quarter
    rest = 2.0 * math.sqrt(2.0) - square
    half_sin = quarter * (rest * lax.rsqrt(rest))
    half_cos = math.sqrt(2.0) - square
    return 1.0 - half_sin * half_sin, half_sin * half_cos


def split(x):
    high = x.astype(BF16)
    return high, (x - high.astype(F32)).astype(BF16)


def dot(a, b, dims):
    return lax.dot_general(a, b, dims, preferred_element_type=F32)


def kernel(
    mil, pos, wts, obs, gw_recv, gp_recv,
    mil_own, mil_use, pos_own, obs_own, obs_row, obs_send, posbuf, wbuf, mil_rows, pos_t, wsplit,
    hi_a, lo_a, hi_b, lo_b, phase,
    amps, shares, coefs, left, grads, gw_send, gp_send,
    in_sem, a_send, a_recv, m_send, m_recv, r_send, r_recv, c_send, c_recv, d_send, d_recv,
    ready, met,
):
    kv, bead = lax.axis_index("kv"), lax.axis_index("bead")
    z_low, x = kv // 4, lax.rem(kv, 4)
    core = lax.rem(bead, 2)
    own = x * 2 + core
    channel = (bead // 8) * 8 + lax.rem(bead // 2, 4) * 2 + z_low
    waves, beads = mil_use.shape[1], pos.shape[1]
    chunks = waves // CHUNK
    chips = SHARERS // 2

    def sharer(g):
        return (z_low * 4 + g // 2, (bead // 2) * 2 + lax.rem(g, 2))

    def reducer(r, to_core):
        y, z = r // 8, lax.rem(r, 8)
        return (lax.rem(z, 2) * 4 + x, (y * 4 + z // 2) * 2 + to_core)

    def others():
        for dy, dz in FAR_FIRST:
            yield lax.rem(channel // 8 + dy, 4) * 8 + lax.rem(channel + dz, 8)

    def remote(src, dst, send, recv, device):
        return pltpu.make_async_remote_copy(
            src_ref=src, dst_ref=dst, send_sem=send, recv_sem=recv, device_id=device, device_id_type=MESH
        )

    def greet(device):
        pl.semaphore_signal(barrier, inc=1, device_id=device, device_id_type=MESH)

    def lanes(g):
        return pl.ds(pl.multiple_of(g * beads, beads), beads)

    barrier = pltpu.get_barrier_semaphore()
    for s in range(1, chips):
        greet(sharer(2 * lax.rem(x + s, chips)))

    @pl.when(core == 1)
    def _():
        greet((kv, bead - 1))

    greet(((1 - z_low) * 4 + x, bead - core))
    inputs = [
        pltpu.make_async_copy(src, dst, in_sem.at[i])
        for i, (src, dst) in enumerate(
            ((pos, pos_own), (wts, wbuf.at[:, lanes(own)]), (mil, mil_own), (obs, obs_own))
        )
    ]
    for copy in inputs:
        copy.start()
    for s in range(1, REDUCERS):
        greet(reducer(lax.rem(channel + s, REDUCERS), 1))
    for copy in inputs:
        copy.wait()

    where = pos_own[...].astype(F32)
    upper = jnp.floor(where * (1.0 / 64.0))
    lower = where - 64.0 * upper
    posbuf[:, lanes(own)] = jnp.concatenate(
        [upper * (1.0 / 64.0), lower * (1.0 / LATTICE), jnp.zeros((2, beads), F32)], 0
    )

    def put_row(ref, row):
        for t in range(waves // 128):
            ref[t : t + 1, :] = row[:, t * 128 : (t + 1) * 128]

    @pl.when(core == 0)
    def _():
        put_row(obs_send, obs_own[pl.ds(channel + 1 - 2 * z_low, 1), :])

    @pl.when(core == z_low)
    def _():
        mil_use[...] = mil_own[...]
        put_row(obs_row, obs_own[pl.ds(channel, 1), :])

    @pl.when(core == 0)
    def _():
        pl.semaphore_wait(barrier, SHARERS - 1 + 2)
        pl.semaphore_signal(ready, inc=1, device_id=(kv, bead + 1), device_id_type=MESH)

    @pl.when(core == 1)
    def _():
        pl.semaphore_wait(ready, 1)

    def pos_copy(s):
        g = lax.rem(own + s, SHARERS)
        at = posbuf.at[:, lanes(own)]
        return remote(at, at, a_send.at[0, s], a_recv.at[0, s], sharer(g))

    def wts_copy(s):
        g = lax.rem(own + s, SHARERS)
        at = wbuf.at[:, lanes(own)]
        return remote(at, at, a_send.at[1, s], a_recv.at[1, s], sharer(g))

    beyond = ((1 - z_low) * 4 + x, bead - core + z_low)
    mil_copy = remote(mil_own, mil_use, m_send.at[0], m_recv.at[0], beyond)
    obs_copy = remote(obs_send, obs_row, m_send.at[1], m_recv.at[1], beyond)

    for s in range(1, SHARERS):
        pos_copy(s).start()

    @pl.when(core == 0)
    def _():
        mil_copy.start()
        obs_copy.start()

    for s in range(1, SHARERS):
        wts_copy(s).start()

    @pl.when(core != z_low)
    def _():
        mil_copy.wait_recv()

    index = mil_use[...].astype(F32)
    mil_rows[...] = jnp.concatenate([index, index, jnp.zeros((2, waves), F32)], 0).astype(BF16)

    sets = ((hi_a, lo_a), (hi_b, lo_b))
    rows = 32

    def share_copy(q, r, to):
        src = amps.at[q, pl.ds(pl.multiple_of(to * PIECE, PIECE), PIECE), :]
        dst = shares.at[q, pl.ds(pl.multiple_of(r * PIECE, PIECE), PIECE), :]
        return remote(src, dst, r_send.at[q], r_recv.at[q], reducer(to, core))

    def coef_copy(q, to):
        at = coefs.at[q, pl.ds(pl.multiple_of(channel * PIECE, PIECE), PIECE), :]
        return remote(at, at, c_send.at[q], c_recv.at[q], reducer(to, core))

    def all_pieces(buf, q, send, recv):
        at = buf.at[q, pl.ds(0, (REDUCERS - 1) * PIECE), :]
        return remote(at, at, send.at[q], recv.at[q], reducer(lax.rem(channel + 1, REDUCERS), core))

    def add(q, turn, base):
        hi, lo = sets[turn]
        at = slice(base, base + 2 * CHUNK)
        both = dot(wsplit[...], hi[:, at], NN)
        amp = both[:CHANNELS] + both[CHANNELS:] + dot(wsplit[:CHANNELS, :], lo[:, at], NN)
        for t in range(PIECE):
            amps[q, pl.ds(t, REDUCERS, stride=PIECE), :] = amp[:, t * 128 : (t + 1) * 128]

    def make(q, turn, base, first=0, count=SHARERS * beads):
        hi, lo = sets[turn]
        phase[0:count, :] = dot(pos_t[pl.ds(first, count), :], mil_rows[:, q * CHUNK : (q + 1) * CHUNK], NN)
        for r in range(0, count, rows):
            to = pl.ds(first + r, rows) if isinstance(first, int) else pl.ds(pl.multiple_of(first + r, rows), rows)
            for part, value in enumerate(cos_sin(phase[r : r + rows, :])):
                at = slice(base + part * CHUNK, base + (part + 1) * CHUNK)
                hi[to, at], lo[to, at] = split(value)

    def send_shares(q):
        for r in others():
            share_copy(q, channel, r).start()
        own_rows = pl.ds(pl.multiple_of(channel * PIECE, PIECE), PIECE)
        shares[q, own_rows, :] = amps[q, own_rows, :]

    for step in (0, 1, 3, 2):
        chip = lax.rem(x + step, chips)
        for c in range(2):
            g = chip * 2 + c
            shift = lax.rem(own - g + SHARERS, SHARERS)
            if step:
                pos_copy(shift).wait_recv()
            else:

                @pl.when(g != own)
                def _():
                    pos_copy(shift).wait_recv()

        here = pl.multiple_of(chip * SLICE, SLICE)
        pos_t[pl.ds(here, SLICE), :] = posbuf[:, pl.ds(here, SLICE)].T.astype(BF16)
        make(0, 0, 0, here, SLICE)

    for s in range(1, SHARERS):
        wts_copy(s).wait_recv()
    high, low = split(wbuf[...])
    wsplit[...] = jnp.concatenate([high, low], 0)

    for q in range(chunks):
        base = (q // 2) * 2 * CHUNK
        add(q, q % 2, base)
        if q + 1 < chunks:
            make(q + 1, (q + 1) % 2, ((q + 1) // 2) * 2 * CHUNK)
        if q == 0:

            @pl.when(core == 1)
            def _():
                pl.semaphore_wait(barrier, 2 * (REDUCERS - 1))
                pl.semaphore_signal(met, inc=1, device_id=(kv, bead - 1), device_id_type=MESH)

            @pl.when(core == 0)
            def _():
                pl.semaphore_wait(met, 1)

        send_shares(q)

    @pl.when(core != z_low)
    def _():
        obs_copy.wait_recv()

    bead_total = float(BEADS)

    def coefficients(q, carry):
        all_pieces(shares, q, r_send, r_recv).wait_recv()
        total = shares[q, 0:8, :]
        for r in range(8, REDUCERS * PIECE, 8):
            total = total + shares[q, r : r + 8, :]
        total = total[:PIECE] + total[PIECE:]
        amp_cos, amp_sin = total[:TILES], total[TILES:]
        measured = obs_row[pl.ds(q * TILES, TILES), :]
        residual = (amp_cos * amp_cos + amp_sin * amp_sin) * (1.0 / bead_total) - measured
        scale = residual * (2.0 / bead_total)
        own_rows = pl.ds(pl.multiple_of(channel * PIECE, PIECE), PIECE)
        coefs[q, own_rows, :] = jnp.concatenate([scale * amp_cos, scale * amp_sin], 0)
        for r in others():
            coef_copy(q, r).start()
        return carry

    lax.fori_loop(0, chunks, coefficients, 0)

    wide = 4 * CHANNELS

    def sum_copies(g, s):
        device = sharer(g)
        return (
            remote(gw_send.at[g], gw_recv.at[own], d_send.at[0, s], d_recv.at[0, s], device),
            remote(gp_send.at[g], gp_recv.at[own], d_send.at[1, s], d_recv.at[1, s], device),
        )

    def backward(h):
        for q in (2 * h, 2 * h + 1):
            all_pieces(coefs, q, c_send, c_recv).wait_recv()
            for t in range(TILES):
                at = slice(q * CHUNK + t * 128, q * CHUNK + (t + 1) * 128)
                co = coefs[q, pl.ds(t, CHANNELS, stride=PIECE), :]
                si = coefs[q, pl.ds(TILES + t, CHANNELS, stride=PIECE), :]
                vec = mil_use[:, at].astype(F32) * (TWO_PI / BOX_LEN)
                for d in range(4):
                    lc, ls = (co, si) if d == 0 else (vec[d - 1 : d] * si, -vec[d - 1 : d] * co)
                    for part, value in ((0, lc), (1, ls)):
                        hi, lo = split(value)
                        first = (2 * (q - 2 * h) + part) * CHUNK + t * 128
                        to = slice(first, first + 128)
                        left[d * CHANNELS : (d + 1) * CHANNELS, to] = hi
                        left[(4 + d) * CHANNELS : (5 + d) * CHANNELS, to] = lo

        span = slice(h * 2 * CHUNK, (h + 1) * 2 * CHUNK)

        def one_chip(i, carry):
            chip = lax.rem(x + 1 + i, chips)
            at = pl.ds(pl.multiple_of(chip * SLICE, SLICE), SLICE)
            both = dot(left[...], jnp.concatenate([hi_a[at, span], hi_b[at, span]], 1), NT)
            rest = dot(left[:wide, :], jnp.concatenate([lo_a[at, span], lo_b[at, span]], 1), NT)
            total = both[:wide] + both[wide:] + rest
            if h > 0:
                total = total + grads[:, at]
            if h < chunks // 2 - 1:
                grads[:, at] = total
                return carry
            weight = wbuf[:, at]
            comps = [
                jnp.sum(weight * total[CHANNELS * (d + 1) : CHANNELS * (d + 2)], 0, keepdims=True) for d in range(3)
            ]
            comps = jnp.concatenate(comps + [jnp.zeros((1, SLICE), F32)], 0)
            for c in range(2):
                g = chip * 2 + c
                gw_send[g] = total[:CHANNELS, c * beads : (c + 1) * beads]
                gp_send[g] = comps[:, c * beads : (c + 1) * beads]

                @pl.when(g != own)
                def _():
                    for copy in sum_copies(g, lax.rem(g - own + SHARERS, SHARERS)):
                        copy.start()

            return carry

        lax.fori_loop(0, chips, one_chip, 0)

    for h in range(chunks // 2):
        backward(h)

    kept = [
        pltpu.make_async_copy(gw_send.at[own], gw_recv.at[own], in_sem.at[0]),
        pltpu.make_async_copy(gp_send.at[own], gp_recv.at[own], in_sem.at[1]),
    ]
    for copy in kept:
        copy.start()
    for s in range(1, SHARERS):
        for copy in sum_copies(lax.rem(own + s, SHARERS), s):
            copy.wait_recv()
    for copy in kept:
        copy.wait()

    for s in range(1, SHARERS):
        pos_copy(s).wait_send()
        wts_copy(s).wait_send()
        for copy in sum_copies(lax.rem(own + s, SHARERS), s):
            copy.wait_send()
    for q in range(chunks):
        all_pieces(amps, q, r_send, r_recv).wait_send()
        all_pieces(coefs, q, c_send, c_recv).wait_send()

    @pl.when(core == 0)
    def _():
        mil_copy.wait_send()
        obs_copy.wait_send()


def total_kernel(gw_parts, gp_parts, gw_out, gp_out):
    gw, gp = gw_parts[0], gp_parts[0]
    for g in range(1, SHARERS):
        gw, gp = gw + gw_parts[g], gp + gp_parts[g]
    gw_out[...] = gw
    gp_out[...] = gp[:3]


def per_device(miller, lattice_pos, weights, observed):
    waves, beads = miller.shape[1], lattice_pos.shape[1]
    many = SHARERS * beads
    chunks = waves // CHUNK
    hbm = pl.BlockSpec(memory_space=pltpu.HBM)
    vmem = pl.BlockSpec(memory_space=pltpu.VMEM)
    dma = pltpu.SemaphoreType.DMA
    pieces = pltpu.VMEM((chunks, REDUCERS * PIECE, 128), F32)
    sent = [pltpu.VMEM((SHARERS, CHANNELS, beads), F32), pltpu.VMEM((SHARERS, 4, beads), F32)]
    parts = pl.pallas_call(
        kernel,
        out_shape=(
            jax.ShapeDtypeStruct((SHARERS, CHANNELS, beads), F32),
            jax.ShapeDtypeStruct((SHARERS, 4, beads), F32),
        ),
        in_specs=[hbm] * 4,
        out_specs=[hbm] * 2,
        scratch_shapes=[
            pltpu.VMEM(miller.shape, jnp.int32),
            pltpu.VMEM(miller.shape, jnp.int32),
            pltpu.VMEM(lattice_pos.shape, jnp.int32),
            pltpu.VMEM(observed.shape, F32),
            pltpu.VMEM((waves // 128, 128), F32),
            pltpu.VMEM((waves // 128, 128), F32),
            pltpu.VMEM((8, many), F32),
            pltpu.VMEM((CHANNELS, many), F32),
            pltpu.VMEM((8, waves), BF16),
            pltpu.VMEM((many, 8), BF16),
            pltpu.VMEM((2 * CHANNELS, many), BF16),
        ]
        + [pltpu.VMEM((many, waves), BF16)] * 4
        + [pltpu.VMEM((many, CHUNK), F32)]
        + [pieces] * 3
        + [pltpu.VMEM((8 * CHANNELS, 4 * CHUNK), BF16), pltpu.VMEM((4 * CHANNELS, many), F32)]
        + sent
        + [
            dma((4,)),
            dma((2, SHARERS)),
            dma((2, SHARERS)),
            dma((2,)),
            dma((2,)),
            dma((chunks,)),
            dma((chunks,)),
            dma((chunks,)),
            dma((chunks,)),
            dma((2, SHARERS)),
            dma((2, SHARERS)),
            pltpu.SemaphoreType.REGULAR,
            pltpu.SemaphoreType.REGULAR,
        ],
        compiler_params=pltpu.CompilerParams(
            collective_id=0, has_side_effects=True, vmem_limit_bytes=56 * 1024 * 1024
        ),
    )(miller, lattice_pos, weights, observed)
    return pl.pallas_call(
        total_kernel,
        out_shape=(
            jax.ShapeDtypeStruct((CHANNELS, beads), F32),
            jax.ShapeDtypeStruct((3, beads), F32),
        ),
        in_specs=[vmem] * 2,
        out_specs=[vmem] * 2,
    )(*parts)


def solution(mesh):
    in_specs = (P(None, "kv"), P(None, ("kv", "bead")), P(None, ("kv", "bead")), P(None, "kv"))
    out_specs = (P(None, ("kv", "bead")), P(None, ("kv", "bead")))
    return jax.shard_map(
        per_device, mesh=mesh, in_specs=in_specs, out_specs=out_specs, check_vma=False
    )
```

```python
import functools
import math

import jax
import jax.numpy as jnp
from jax import lax
from jax.experimental import pallas as pl
from jax.experimental.pallas import tpu as pltpu
from jax.sharding import PartitionSpec as P

CHANNELS = 32
LATTICE = 4096
BOX_LEN = 64
BEADS = 32768
TWO_PI = 2.0 * math.pi
MESH = pl.DeviceIdType.MESH
BF16 = jnp.bfloat16
F32 = jnp.float32

SIN_POLY = (2.641753911972046, -1.0863758325576782, 0.13399836421012878, -0.0077232783660292625)

SHARERS = 8
REDUCERS = 32
CHUNK = 256
SLICE = 256
TILES = CHUNK // 128
PIECE = 2 * TILES
NT = (((1,), (1,)), ((), ()))
NN = (((1,), (0,)), ((), ()))


FAR_FIRST = sorted(
    ((dy, dz) for dy in range(4) for dz in range(8) if dy or dz),
    key=lambda step: -min(step[0], 4 - step[0]) - min(step[1], 8 - step[1]),
)


def poly(u, coefs):
    total = u * coefs[-1] + coefs[-2]
    for c in coefs[-3::-1]:
        total = total * u + c
    return total


def cos_sin(turns):
    f = turns - jnp.round(turns)
    quarter = poly(f * f, SIN_POLY) * f
    square = quarter * quarter
    rest = 2.0 * math.sqrt(2.0) - square
    half_sin = quarter * (rest * lax.rsqrt(rest))
    half_cos = math.sqrt(2.0) - square
    return 1.0 - half_sin * half_sin, half_sin * half_cos


def split(x):
    high = x.astype(BF16)
    return high, (x - high.astype(F32)).astype(BF16)


def dot(a, b, dims):
    return lax.dot_general(a, b, dims, preferred_element_type=F32)


def kernel(
    mil, pos, wts, obs, gw_recv, gp_recv,
    mil_own, mil_use, pos_own, obs_own, obs_row, obs_send, posbuf, wbuf, mil_rows, pos_t, wsplit,
    hi_a, lo_a, hi_b, lo_b, phase,
    amps, shares, coefs, left, grads, gw_send, gp_send,
    in_sem, a_send, a_recv, m_send, m_recv, r_send, r_recv, c_send, c_recv, d_send, d_recv,
    ready, met,
):
    kv, bead = lax.axis_index("kv"), lax.axis_index("bead")
    z_low, x = kv // 4, lax.rem(kv, 4)
    core = lax.rem(bead, 2)
    own = x * 2 + core
    channel = (bead // 8) * 8 + lax.rem(bead // 2, 4) * 2 + z_low
    waves, beads = mil_use.shape[1], pos.shape[1]
    chunks = waves // CHUNK
    chips = SHARERS // 2

    def sharer(g):
        return (z_low * 4 + g // 2, (bead // 2) * 2 + lax.rem(g, 2))

    def reducer(r, to_core):
        y, z = r // 8, lax.rem(r, 8)
        return (lax.rem(z, 2) * 4 + x, (y * 4 + z // 2) * 2 + to_core)

    def others():
        for dy, dz in FAR_FIRST:
            yield lax.rem(channel // 8 + dy, 4) * 8 + lax.rem(channel + dz, 8)

    def remote(src, dst, send, recv, device):
        return pltpu.make_async_remote_copy(
            src_ref=src, dst_ref=dst, send_sem=send, recv_sem=recv, device_id=device, device_id_type=MESH
        )

    def greet(device):
        pl.semaphore_signal(barrier, inc=1, device_id=device, device_id_type=MESH)

    def lanes(g):
        return pl.ds(pl.multiple_of(g * beads, beads), beads)

    barrier = pltpu.get_barrier_semaphore()
    for s in range(1, chips):
        greet(sharer(2 * lax.rem(x + s, chips)))

    @pl.when(core == 1)
    def _():
        greet((kv, bead - 1))

    greet(((1 - z_low) * 4 + x, bead - core))
    inputs = [
        pltpu.make_async_copy(src, dst, in_sem.at[i])
        for i, (src, dst) in enumerate(
            ((pos, pos_own), (wts, wbuf.at[:, lanes(own)]), (mil, mil_own), (obs, obs_own))
        )
    ]
    for copy in inputs:
        copy.start()
    for s in range(1, REDUCERS):
        greet(reducer(lax.rem(channel + s, REDUCERS), 1))
    for copy in inputs:
        copy.wait()

    where = pos_own[...].astype(F32)
    upper = jnp.floor(where * (1.0 / 64.0))
    lower = where - 64.0 * upper
    posbuf[:, lanes(own)] = jnp.concatenate(
        [upper * (1.0 / 64.0), lower * (1.0 / LATTICE), jnp.zeros((2, beads), F32)], 0
    )

    def put_row(ref, row):
        for t in range(waves // 128):
            ref[t : t + 1, :] = row[:, t * 128 : (t + 1) * 128]

    @pl.when(core == 0)
    def _():
        put_row(obs_send, obs_own[pl.ds(channel + 1 - 2 * z_low, 1), :])

    @pl.when(core == z_low)
    def _():
        mil_use[...] = mil_own[...]
        put_row(obs_row, obs_own[pl.ds(channel, 1), :])

    @pl.when(core == 0)
    def _():
        pl.semaphore_wait(barrier, SHARERS - 1 + 2)
        pl.semaphore_signal(ready, inc=1, device_id=(kv, bead + 1), device_id_type=MESH)

    @pl.when(core == 1)
    def _():
        pl.semaphore_wait(ready, 1)

    def pos_copy(s):
        g = lax.rem(own + s, SHARERS)
        at = posbuf.at[:, lanes(own)]
        return remote(at, at, a_send.at[0, s], a_recv.at[0, s], sharer(g))

    def wts_copy(s):
        g = lax.rem(own + s, SHARERS)
        at = wbuf.at[:, lanes(own)]
        return remote(at, at, a_send.at[1, s], a_recv.at[1, s], sharer(g))

    beyond = ((1 - z_low) * 4 + x, bead - core + z_low)
    mil_copy = remote(mil_own, mil_use, m_send.at[0], m_recv.at[0], beyond)
    obs_copy = remote(obs_send, obs_row, m_send.at[1], m_recv.at[1], beyond)

    @pl.when(core == 0)
    def _():
        mil_copy.start()
        obs_copy.start()

    for s in range(1, SHARERS):
        pos_copy(s).start()

    for s in range(1, SHARERS):
        wts_copy(s).start()

    @pl.when(core != z_low)
    def _():
        mil_copy.wait_recv()

    index = mil_use[...].astype(F32)
    mil_rows[...] = jnp.concatenate([index, index, jnp.zeros((2, waves), F32)], 0).astype(BF16)

    sets = ((hi_a, lo_a), (hi_b, lo_b))
    rows = 32

    def share_copy(q, r, to):
        src = amps.at[q, pl.ds(pl.multiple_of(to * PIECE, PIECE), PIECE), :]
        dst = shares.at[q, pl.ds(pl.multiple_of(r * PIECE, PIECE), PIECE), :]
        return remote(src, dst, r_send.at[q], r_recv.at[q], reducer(to, core))

    def coef_copy(q, to):
        at = coefs.at[q, pl.ds(pl.multiple_of(channel * PIECE, PIECE), PIECE), :]
        return remote(at, at, c_send.at[q], c_recv.at[q], reducer(to, core))

    def all_pieces(buf, q, send, recv):
        at = buf.at[q, pl.ds(0, (REDUCERS - 1) * PIECE), :]
        return remote(at, at, send.at[q], recv.at[q], reducer(lax.rem(channel + 1, REDUCERS), core))

    def add(q, turn, base):
        hi, lo = sets[turn]
        at = slice(base, base + 2 * CHUNK)
        both = dot(wsplit[...], hi[:, at], NN)
        amp = both[:CHANNELS] + both[CHANNELS:] + dot(wsplit[:CHANNELS, :], lo[:, at], NN)
        for t in range(PIECE):
            amps[q, pl.ds(t, REDUCERS, stride=PIECE), :] = amp[:, t * 128 : (t + 1) * 128]

    def make(q, turn, base, first=0, count=SHARERS * beads):
        hi, lo = sets[turn]
        phase[0:count, :] = dot(pos_t[pl.ds(first, count), :], mil_rows[:, q * CHUNK : (q + 1) * CHUNK], NN)
        for r in range(0, count, rows):
            to = pl.ds(first + r, rows) if isinstance(first, int) else pl.ds(pl.multiple_of(first + r, rows), rows)
            for part, value in enumerate(cos_sin(phase[r : r + rows, :])):
                at = slice(base + part * CHUNK, base + (part + 1) * CHUNK)
                hi[to, at], lo[to, at] = split(value)

    def send_shares(q):
        for r in others():
            share_copy(q, channel, r).start()
        own_rows = pl.ds(pl.multiple_of(channel * PIECE, PIECE), PIECE)
        shares[q, own_rows, :] = amps[q, own_rows, :]

    for step in (0, 1, 3, 2):
        chip = lax.rem(x + step, chips)
        for c in range(2):
            g = chip * 2 + c
            shift = lax.rem(own - g + SHARERS, SHARERS)
            if step:
                pos_copy(shift).wait_recv()
            else:

                @pl.when(g != own)
                def _():
                    pos_copy(shift).wait_recv()

        here = pl.multiple_of(chip * SLICE, SLICE)
        pos_t[pl.ds(here, SLICE), :] = posbuf[:, pl.ds(here, SLICE)].T.astype(BF16)
        make(0, 0, 0, here, SLICE)

    for s in range(1, SHARERS):
        wts_copy(s).wait_recv()
    high, low = split(wbuf[...])
    wsplit[...] = jnp.concatenate([high, low], 0)

    for q in range(chunks):
        base = (q // 2) * 2 * CHUNK
        add(q, q % 2, base)
        if q + 1 < chunks:
            make(q + 1, (q + 1) % 2, ((q + 1) // 2) * 2 * CHUNK)
        if q == 0:

            @pl.when(core == 1)
            def _():
                pl.semaphore_wait(barrier, 2 * (REDUCERS - 1))
                pl.semaphore_signal(met, inc=1, device_id=(kv, bead - 1), device_id_type=MESH)

            @pl.when(core == 0)
            def _():
                pl.semaphore_wait(met, 1)

        send_shares(q)

    @pl.when(core != z_low)
    def _():
        obs_copy.wait_recv()

    bead_total = float(BEADS)

    def coefficients(q, carry):
        all_pieces(shares, q, r_send, r_recv).wait_recv()
        total = shares[q, 0:8, :]
        for r in range(8, REDUCERS * PIECE, 8):
            total = total + shares[q, r : r + 8, :]
        total = total[:PIECE] + total[PIECE:]
        amp_cos, amp_sin = total[:TILES], total[TILES:]
        measured = obs_row[pl.ds(q * TILES, TILES), :]
        residual = (amp_cos * amp_cos + amp_sin * amp_sin) * (1.0 / bead_total) - measured
        scale = residual * (2.0 / bead_total)
        own_rows = pl.ds(pl.multiple_of(channel * PIECE, PIECE), PIECE)
        coefs[q, own_rows, :] = jnp.concatenate([scale * amp_cos, scale * amp_sin], 0)
        for r in others():
            coef_copy(q, r).start()
        return carry

    lax.fori_loop(0, chunks, coefficients, 0)

    wide = 4 * CHANNELS

    def sum_copies(g, s):
        device = sharer(g)
        return (
            remote(gw_send.at[g], gw_recv.at[own], d_send.at[0, s], d_recv.at[0, s], device),
            remote(gp_send.at[g], gp_recv.at[own], d_send.at[1, s], d_recv.at[1, s], device),
        )

    def backward(h):
        for q in (2 * h, 2 * h + 1):
            all_pieces(coefs, q, c_send, c_recv).wait_recv()
            for t in range(TILES):
                at = slice(q * CHUNK + t * 128, q * CHUNK + (t + 1) * 128)
                co = coefs[q, pl.ds(t, CHANNELS, stride=PIECE), :]
                si = coefs[q, pl.ds(TILES + t, CHANNELS, stride=PIECE), :]
                vec = mil_use[:, at].astype(F32) * (TWO_PI / BOX_LEN)
                for d in range(4):
                    lc, ls = (co, si) if d == 0 else (vec[d - 1 : d] * si, -vec[d - 1 : d] * co)
                    for part, value in ((0, lc), (1, ls)):
                        hi, lo = split(value)
                        first = (2 * (q - 2 * h) + part) * CHUNK + t * 128
                        to = slice(first, first + 128)
                        left[d * CHANNELS : (d + 1) * CHANNELS, to] = hi
                        left[(4 + d) * CHANNELS : (5 + d) * CHANNELS, to] = lo

        span = slice(h * 2 * CHUNK, (h + 1) * 2 * CHUNK)

        def one_chip(i, carry):
            chip = lax.rem(x + 1 + i, chips)
            at = pl.ds(pl.multiple_of(chip * SLICE, SLICE), SLICE)
            both = dot(left[...], jnp.concatenate([hi_a[at, span], hi_b[at, span]], 1), NT)
            rest = dot(left[:wide, :], jnp.concatenate([lo_a[at, span], lo_b[at, span]], 1), NT)
            total = both[:wide] + both[wide:] + rest
            if h > 0:
                total = total + grads[:, at]
            if h < chunks // 2 - 1:
                grads[:, at] = total
                return carry
            weight = wbuf[:, at]
            comps = [
                jnp.sum(weight * total[CHANNELS * (d + 1) : CHANNELS * (d + 2)], 0, keepdims=True) for d in range(3)
            ]
            comps = jnp.concatenate(comps + [jnp.zeros((1, SLICE), F32)], 0)
            for c in range(2):
                g = chip * 2 + c
                gw_send[g] = total[:CHANNELS, c * beads : (c + 1) * beads]
                gp_send[g] = comps[:, c * beads : (c + 1) * beads]

                @pl.when(g != own)
                def _():
                    for copy in sum_copies(g, lax.rem(g - own + SHARERS, SHARERS)):
                        copy.start()

            return carry

        lax.fori_loop(0, chips, one_chip, 0)

    for h in range(chunks // 2):
        backward(h)

    kept = [
        pltpu.make_async_copy(gw_send.at[own], gw_recv.at[own], in_sem.at[0]),
        pltpu.make_async_copy(gp_send.at[own], gp_recv.at[own], in_sem.at[1]),
    ]
    for copy in kept:
        copy.start()
    for s in range(1, SHARERS):
        for copy in sum_copies(lax.rem(own + s, SHARERS), s):
            copy.wait_recv()
    for copy in kept:
        copy.wait()

    for s in range(1, SHARERS):
        pos_copy(s).wait_send()
        wts_copy(s).wait_send()
        for copy in sum_copies(lax.rem(own + s, SHARERS), s):
            copy.wait_send()
    for q in range(chunks):
        all_pieces(amps, q, r_send, r_recv).wait_send()
        all_pieces(coefs, q, c_send, c_recv).wait_send()

    @pl.when(core == 0)
    def _():
        mil_copy.wait_send()
        obs_copy.wait_send()


def total_kernel(gw_parts, gp_parts, gw_out, gp_out):
    gw, gp = gw_parts[0], gp_parts[0]
    for g in range(1, SHARERS):
        gw, gp = gw + gw_parts[g], gp + gp_parts[g]
    gw_out[...] = gw
    gp_out[...] = gp[:3]


def per_device(miller, lattice_pos, weights, observed):
    waves, beads = miller.shape[1], lattice_pos.shape[1]
    many = SHARERS * beads
    chunks = waves // CHUNK
    hbm = pl.BlockSpec(memory_space=pltpu.HBM)
    vmem = pl.BlockSpec(memory_space=pltpu.VMEM)
    dma = pltpu.SemaphoreType.DMA
    pieces = pltpu.VMEM((chunks, REDUCERS * PIECE, 128), F32)
    sent = [pltpu.VMEM((SHARERS, CHANNELS, beads), F32), pltpu.VMEM((SHARERS, 4, beads), F32)]
    parts = pl.pallas_call(
        kernel,
        out_shape=(
            jax.ShapeDtypeStruct((SHARERS, CHANNELS, beads), F32),
            jax.ShapeDtypeStruct((SHARERS, 4, beads), F32),
        ),
        in_specs=[hbm] * 4,
        out_specs=[hbm] * 2,
        scratch_shapes=[
            pltpu.VMEM(miller.shape, jnp.int32),
            pltpu.VMEM(miller.shape, jnp.int32),
            pltpu.VMEM(lattice_pos.shape, jnp.int32),
            pltpu.VMEM(observed.shape, F32),
            pltpu.VMEM((waves // 128, 128), F32),
            pltpu.VMEM((waves // 128, 128), F32),
            pltpu.VMEM((8, many), F32),
            pltpu.VMEM((CHANNELS, many), F32),
            pltpu.VMEM((8, waves), BF16),
            pltpu.VMEM((many, 8), BF16),
            pltpu.VMEM((2 * CHANNELS, many), BF16),
        ]
        + [pltpu.VMEM((many, waves), BF16)] * 4
        + [pltpu.VMEM((many, CHUNK), F32)]
        + [pieces] * 3
        + [pltpu.VMEM((8 * CHANNELS, 4 * CHUNK), BF16), pltpu.VMEM((4 * CHANNELS, many), F32)]
        + sent
        + [
            dma((4,)),
            dma((2, SHARERS)),
            dma((2, SHARERS)),
            dma((2,)),
            dma((2,)),
            dma((chunks,)),
            dma((chunks,)),
            dma((chunks,)),
            dma((chunks,)),
            dma((2, SHARERS)),
            dma((2, SHARERS)),
            pltpu.SemaphoreType.REGULAR,
            pltpu.SemaphoreType.REGULAR,
        ],
        compiler_params=pltpu.CompilerParams(
            collective_id=0, has_side_effects=True, vmem_limit_bytes=56 * 1024 * 1024
        ),
    )(miller, lattice_pos, weights, observed)
    return pl.pallas_call(
        total_kernel,
        out_shape=(
            jax.ShapeDtypeStruct((CHANNELS, beads), F32),
            jax.ShapeDtypeStruct((3, beads), F32),
        ),
        in_specs=[vmem] * 2,
        out_specs=[vmem] * 2,
    )(*parts)


def solution(mesh):
    in_specs = (P(None, "kv"), P(None, ("kv", "bead")), P(None, ("kv", "bead")), P(None, "kv"))
    out_specs = (P(None, ("kv", "bead")), P(None, ("kv", "bead")))
    return jax.shard_map(
        per_device, mesh=mesh, in_specs=in_specs, out_specs=out_specs, check_vma=False
    )
```
